512 devices in a mesh: gx: 16 (over x, y), gy: 32 (over z, core).
Axes of the slice: x: 4, y: 4, z: 16, core: 2. Of those that a mesh axis runs over, the one named last changes fastest.
Arguments:
- conc: float32 [512, 256, 1024], P('gy', 'gx'), may hold values from 0.05 to 2
- target_one: float32 [512, 256, 1024], P('gy', 'gx'), may hold values from 0.05 to 5
- target_two: float32 [512, 256, 1024], P('gy', 'gx'), may hold values from 0.05 to 5
- diffusivity: float32 [512], replicated, may hold values from 2 to 200
- src_shift: int32 [512, 256, 8], P('gy', 'gx'), may hold values from 0 to 2, as said below
- src_tile: int32 [512, 256, 8], P('gy', 'gx'), may hold values from 0 to 2047
- interp_class: int32 [512, 256, 8], P('gy', 'gx'), may hold values from 0 to 7
- interp_mats: float32 [8, 128, 128], replicated, may hold values from 0 to 1, as said below
Outputs:
- new_conc: float32 [512, 256, 1024], P('gy', 'gx')
The draws below stay inside these ranges and needn't reach their ends.
Inputs may be any that keep to these rules, and one draw needn't show every extreme that they name: `src_shift`: on the device at gx index i every offset is at most i; on each device at most 512 tiles have offset 1 and at most 512 have offset 2, and some device has exactly 512 of each. `interp_mats`: each matrix is tridiagonal with nonnegative entries.
All inputs are finite; a program needn't handle non-finite values.
Results may differ from the reference program's by a relative error of at most 0.00025.
Values sent between devices are 32-bit elements; how exact they have to be, the bound alone decides.
No kernel may reach another device: no remote copies, remote signals or barrier semaphores. Data moves between devices by JAX's collectives and lax.ppermute only.
A program may use at most 64 MiB of HBM per device.

```python
import math
import jax
import jax.numpy as jnp
from jax import lax

NZ = 512
TILE = 128
NMAT = 8
CX = 16
NY = 1024
NX = 256
ZS = 16
NB = 8
N_GX = 16
N_GY = 32


def draw_src_shift(key, part):
    tile_count = CX * ZS * NB
    capacity = max(2, tile_count // 4)
    first_key, busy_key, column_key, order_key = jax.random.split(key, 4)
    levels = jax.random.randint(first_key, (2, N_GX, N_GY), 0, 4)
    counts = jnp.right_shift(jnp.full((2, N_GX, N_GY), capacity, jnp.int32), levels)
    busy_x = jax.random.randint(busy_key, (), 2, N_GX)
    busy_y = jax.random.randint(column_key, (), 0, N_GY)
    counts = counts.at[:, busy_x, busy_y].set(capacity)
    allowed = jnp.arange(N_GX, dtype=jnp.int32)[None, :, None] >= jnp.array([1, 2], jnp.int32)[:, None, None]
    counts = jnp.where(allowed, counts, 0)
    device_keys = jax.random.split(order_key, N_GX * N_GY)
    rank_order = jax.vmap(lambda one_key: jax.random.permutation(one_key, tile_count))(device_keys)
    rank_order = rank_order.reshape(N_GX, N_GY, tile_count).astype(jnp.int32)
    first_count = counts[0][:, :, None]
    second_count = counts[1][:, :, None]
    offsets = jnp.where(rank_order < first_count, 1, jnp.where(rank_order < first_count + second_count, 2, 0)).astype(jnp.int32)
    offsets = offsets.reshape(N_GX, N_GY, ZS, CX, NB).transpose(1, 2, 0, 3, 4)
    return offsets.reshape(NZ, CX * N_GX, NB)


def draw_interp_mats(key, part):
    first_key, second_key, third_key = jax.random.split(key, 3)
    diagonal = jax.random.uniform(first_key, (NMAT, TILE), jnp.float32, 0.6, 0.8)
    below_part = jax.random.uniform(second_key, (NMAT, TILE), jnp.float32, 0.12, 0.28)
    above_part = jax.random.uniform(third_key, (NMAT, TILE), jnp.float32, 0.12, 0.28)
    identity = jnp.eye(TILE, dtype=jnp.float32)
    below_band = jnp.eye(TILE, k=-1, dtype=jnp.float32)
    above_band = jnp.eye(TILE, k=1, dtype=jnp.float32)
    return diagonal[:, :, None] * identity + below_part[:, :, None] * below_band + above_part[:, :, None] * above_band


def touch_ends(result, own_key, low, largest):
    place = [jax.random.randint(jax.random.fold_in(own_key, axis), (), 0, length) for axis, length in enumerate(result.shape)]
    longest = result.shape.index(max(result.shape))
    next_to = place[:longest] + [(place[longest] + 1) % result.shape[longest]] + place[longest + 1:]
    return result.at[tuple(place)].set(low).at[tuple(next_to)].set(largest)


def block_levels(key, dims, shards, smallest, top_value):
    factor_of, own = 1.0, jax.random.fold_in(key, 6)
    for dim, shards_of in shards:
        draws = jnp.exp(jax.random.uniform(jax.random.fold_in(own, dim), (shards_of,), jnp.float32, smallest / len(shards), top_value / len(shards)))
        factor_of = factor_of * jnp.repeat(draws, dims[dim] // shards_of).reshape([-1 if axis == dim else 1 for axis in range(len(dims))])
    return factor_of


def setup_inputs(seed: int = 0) -> dict:
    splits = jax.random.split(jax.random.key(seed), 9)
    return {
        "conc": jnp.clip(jnp.exp(math.log(2.0) - 3.6888794 * jax.random.uniform(splits[0], (NZ, NX, NY), jnp.float32) ** block_levels(splits[0], (NZ, NX, NY), ((0, 32), (1, 16)), -0.2, 0.2)), 0.05, 2.0),
        "target_one": jnp.clip(jnp.exp(math.log(5.0) - 4.6051702 * jax.random.uniform(splits[1], (NZ, NX, NY), jnp.float32) ** block_levels(splits[1], (NZ, NX, NY), ((0, 32), (1, 16)), -0.2, 0.2)), 0.05, 5.0),
        "target_two": jnp.clip(jnp.exp(math.log(5.0) - 4.6051702 * jax.random.uniform(splits[2], (NZ, NX, NY), jnp.float32) ** block_levels(splits[2], (NZ, NX, NY), ((0, 32), (1, 16)), -0.2, 0.2)), 0.05, 5.0),
        "diffusivity": jnp.clip(jnp.exp(jax.random.uniform(splits[3], (NZ,), jnp.float32, math.log(2.0), math.log(200.0))), 2.0, 200.0),
        "src_shift": draw_src_shift(jax.random.fold_in(splits[8], 71), 0),
        "src_tile": touch_ends(jax.random.randint(splits[5], (NZ, NX, NB), 0, CX * ZS * NB), jax.random.fold_in(splits[5], 1), 0, (CX * ZS * NB) - 1).astype(jnp.int32),
        "interp_class": touch_ends(jax.random.randint(splits[6], (NZ, NX, NB), 0, NMAT), jax.random.fold_in(splits[6], 1), 0, NMAT - 1).astype(jnp.int32),
        "interp_mats": draw_interp_mats(jax.random.fold_in(splits[8], 71), 0),
    }


def reference(conc, target_one, target_two, diffusivity, src_shift, src_tile, interp_class, interp_mats):
    z_cells, x_cells, y_cells = conc.shape
    y_blocks = y_cells // TILE
    z_slab = z_cells // N_GY
    x_slab = x_cells // N_GX
    z_index = jnp.arange(z_cells, dtype=jnp.int32)[:, None, None]
    x_index = jnp.arange(x_cells, dtype=jnp.int32)[None, :, None]
    src_z = (z_index // z_slab * z_slab + src_tile // (x_slab * y_blocks)).astype(jnp.int32)
    src_x = ((x_index // x_slab - src_shift) * x_slab + src_tile // y_blocks % x_slab).astype(jnp.int32)
    src_b = (src_tile % y_blocks).astype(jnp.int32)
    tile_rows = conc.reshape(z_cells, x_cells, y_blocks, TILE)
    departed = tile_rows[src_z, src_x, src_b]
    flat_rows = departed.reshape(-1, TILE)
    classes = interp_class.reshape(-1)
    advected = jnp.zeros_like(flat_rows)
    for which_matrix in range(NMAT):
        interpolated = jnp.dot(flat_rows.astype(jnp.float32), interp_mats[which_matrix].T.astype(jnp.float32), precision=lax.Precision.HIGHEST, preferred_element_type=jnp.float32)
        advected = jnp.where((classes == which_matrix)[:, None], interpolated, advected)
    advected = advected.reshape(z_cells, x_cells, y_cells)
    free_part = advected / (1.0 + target_one / (0.5 + advected) + target_two / (2.0 + advected))
    face_coef = 0.5 * (diffusivity[1:] + diffusivity[:-1])
    zero_pad = jnp.zeros((1,), diffusivity.dtype)
    lower_band = jnp.concatenate([zero_pad, -face_coef])
    upper_band = jnp.concatenate([-face_coef, zero_pad])
    main_band = 1.0 + jnp.concatenate([zero_pad, face_coef]) + jnp.concatenate([face_coef, zero_pad])
    solved = lax.linalg.tridiagonal_solve(lower_band, main_band, upper_band, free_part.reshape(z_cells, x_cells * y_cells))
    solved = solved.reshape(z_cells, x_cells, y_cells)
    return solved + (advected - free_part)
```

```python
import functools

import jax
import jax.numpy as jnp
from jax import lax
from jax.experimental import pallas as pl
from jax.experimental.pallas import tpu as pltpu
from jax.sharding import PartitionSpec as P

LANES = 128
NMAT = 8
PLANES = 16
ROWS = 128
TILES = PLANES * ROWS
CAP = 512
HIGH = lax.Precision.HIGHEST
VMEM = pltpu.VMEM
SMEM = pltpu.SMEM


def shifted(value, axis, by):
    peers = lax.axis_size(axis)
    pairs = [(i, i + by) for i in range(peers) if 0 <= i + by < peers]
    return lax.ppermute(value, axis, pairs)


def to_rows(value):
    z, x, y = value.shape
    value = value.reshape(z, x // 8, 8, y // LANES, LANES).transpose(0, 1, 3, 2, 4)
    return value.reshape(z * x * (y // LANES), LANES)


def from_rows(rows, shape):
    z, x, y = shape
    rows = rows.reshape(z, x // 8, y // LANES, 8, LANES).transpose(0, 1, 3, 2, 4)
    return rows.reshape(shape)


def tile_order(value):
    z, x, b = value.shape
    return value.reshape(z, x // 8, 8, b).transpose(0, 1, 3, 2).reshape(z, x * b)


def iota(shape, axis):
    return lax.broadcasted_iota(jnp.int32, shape, axis)


def request_kernel(code_ref, list1_ref, list2_ref, where_ref, picked_ref):
    code = code_ref[...]
    shift = lax.shift_right_logical(code, 11)
    tile = jnp.bitwise_and(code, TILES - 1)
    before_lane = (iota((LANES, LANES), 0) < iota((LANES, LANES), 1)).astype(jnp.bfloat16)
    before_row = (iota((PLANES, PLANES), 1) < iota((PLANES, PLANES), 0)).astype(jnp.bfloat16)
    all_lanes = jnp.ones((LANES, LANES), jnp.bfloat16)
    tile_f = tile.astype(jnp.float32)
    where = tile
    for step, list_ref in ((1, list1_ref), (2, list2_ref)):
        mine = shift == step
        mask = jnp.where(mine, 1.0, 0.0).astype(jnp.bfloat16)
        inside = jnp.dot(mask, before_lane, preferred_element_type=jnp.float32)
        per_row = jnp.dot(mask, all_lanes, preferred_element_type=jnp.float32)
        ahead = jnp.dot(before_row, per_row.astype(jnp.bfloat16), preferred_element_type=jnp.float32)
        rank = (inside + ahead).astype(jnp.int32)
        where = jnp.where(mine, TILES + (step - 1) * CAP + rank, where)
        rank = jnp.where(mine, rank, -1)
        for block in range(CAP // 64):
            slot = iota((64, LANES), 0) + 64 * block
            picked = jnp.zeros((64, LANES), jnp.float32)
            for row in range(PLANES):
                picked = jnp.where(rank[row : row + 1, :] == slot, tile_f[row : row + 1, :], picked)
            picked_ref[pl.ds(64 * block, 64), :] = picked
        total = lax.dot_general(
            jnp.ones((8, LANES), jnp.float32), picked_ref[...], (((1,), (1,)), ((), ())),
            precision=HIGH, preferred_element_type=jnp.float32,
        )
        list_ref[...] = total[0:1, :].astype(jnp.int32)
    where_ref[...] = where


def request(code):
    return pl.pallas_call(
        request_kernel,
        out_shape=(
            jax.ShapeDtypeStruct((1, CAP), jnp.int32),
            jax.ShapeDtypeStruct((1, CAP), jnp.int32),
            jax.ShapeDtypeStruct((PLANES, LANES), jnp.int32),
        ),
        in_specs=[pl.BlockSpec(memory_space=VMEM)],
        out_specs=[pl.BlockSpec(memory_space=VMEM)] * 3,
        scratch_shapes=[pltpu.VMEM((CAP, LANES), jnp.float32)],
        name="request",
    )(code)


def serve_kernel(list1_ref, list2_ref, rows_ref, out1_ref, out2_ref):
    for list_ref, out_ref in ((list1_ref, out1_ref), (list2_ref, out2_ref)):

        def step(k, carry, list_ref=list_ref, out_ref=out_ref):
            for j in range(32):
                slot = k * 32 + j
                out_ref[pl.ds(slot, 1), :] = rows_ref[pl.ds(list_ref[0, slot], 1), :]
            return carry

        lax.fori_loop(0, CAP // 32, step, 0)


def serve(list1, list2, rows):
    out = jax.ShapeDtypeStruct((CAP, LANES), jnp.float32)
    return pl.pallas_call(
        serve_kernel,
        out_shape=(out, out),
        in_specs=[pl.BlockSpec(memory_space=SMEM)] * 2 + [pl.BlockSpec(memory_space=VMEM)],
        out_specs=[pl.BlockSpec(memory_space=VMEM)] * 2,
        name="serve",
    )(list1, list2, rows)


def coef_kernel(kl_ref, kr_ref, mine_ref, mats_ref, own_ref, red_ref, diag_ref, own_t, row_t):
    devices = red_ref.shape[1]
    kl, kr = kl_ref[...], kr_ref[...]
    main = 1.0 + kl + kr
    row = lambda a, z: a[z : z + 1, :]
    inv, low, up = [], [], []
    for z in range(PLANES):
        pivot = row(main, z) if z == 0 else row(main, z) - row(kr, z - 1) * low_up
        inv.append(1.0 / pivot)
        low.append(jnp.zeros_like(pivot) if z == 0 else row(kr, z - 1) * inv[z])
        up.append(row(kr, z) * inv[z])
        low_up = up[z]
    left = [row(kl, 0) * inv[0]]
    for z in range(1, PLANES):
        left.append(low[z] * left[z - 1])
    right = [None] * PLANES
    right[-1] = row(kr, PLANES - 1) * inv[-1]
    for z in range(PLANES - 2, -1, -1):
        left[z] = left[z] + up[z] * left[z + 1]
        right[z] = up[z] * right[z + 1]
    mine = mine_ref[...]
    ones = jnp.ones((LANES, LANES), jnp.float32)
    for kind, values in enumerate((inv, low, up, left, right)):
        for z in range(PLANES):
            own_t[pl.ds(kind * PLANES + z, 1), :] = jnp.where(mine > 0.0, values[z], 0.0)
    own_ref[...] = jnp.dot(own_t[...], ones, precision=HIGH, preferred_element_type=jnp.float32)
    eye = iota((devices, LANES), 0) == iota((devices, LANES), 1)
    for kind, value in enumerate((left[0], left[-1], right[0], right[-1])):
        row_t[pl.ds(kind * devices, devices), :] = jnp.where(eye, value, 0.0)
    spread = jnp.dot(row_t[...], ones, precision=HIGH, preferred_element_type=jnp.float32)
    ratio = jnp.zeros((1, LANES), jnp.float32)
    for d in range(devices):
        l_first, l_last, r_first, r_last = (row(spread, kind * devices + d) for kind in range(4))
        gain = 1.0 / (1.0 - l_first * ratio)
        for kind, value in enumerate(
            (l_last * ratio * gain, l_last * gain, gain, gain * l_first, gain * r_first, ratio)
        ):
            red_ref[kind, pl.ds(d, 1), :] = value
        ratio = r_last + l_last * ratio * gain * r_first
    r, c = iota((LANES, LANES), 0), iota((LANES, LANES), 1)
    diag_ref[...] = jnp.zeros_like(diag_ref)
    for kind, at in enumerate((r == c, r == c + 1, r == c - 1)):
        lanes = pl.ds(kind * LANES, LANES)
        values = jnp.concatenate(
            [jnp.sum(jnp.where(at, mats_ref[m], 0.0), axis=0, keepdims=True) for m in range(NMAT)], axis=0
        )
        first = values.astype(jnp.bfloat16).astype(jnp.float32)
        second = (values - first).astype(jnp.bfloat16).astype(jnp.float32)
        third = values - first - second
        stacked = jnp.concatenate([first, second, third, jnp.zeros_like(first)], axis=0)
        diag_ref[:, lanes] = stacked.astype(jnp.bfloat16)


def coefficients(kl, kr, mine, mats, devices):
    return pl.pallas_call(
        coef_kernel,
        out_shape=(
            jax.ShapeDtypeStruct((5 * PLANES, LANES), jnp.float32),
            jax.ShapeDtypeStruct((6, devices, LANES), jnp.float32),
            jax.ShapeDtypeStruct((4 * NMAT, 3 * LANES), jnp.bfloat16),
        ),
        in_specs=[pl.BlockSpec(memory_space=VMEM)] * 4,
        out_specs=[pl.BlockSpec(memory_space=VMEM)] * 3,
        scratch_shapes=[
            pltpu.VMEM((5 * PLANES, LANES), jnp.float32),
            pltpu.VMEM((4 * devices, LANES), jnp.float32),
        ],
        name="coefficients",
    )(kl, kr, mine, mats)


def slab_kernel(
    where_ref, rows_hbm, got1_hbm, got2_hbm, one_ref, two_ref, class_ref, diag_ref, own_ref,
    base_ref, ends_ref, src, dep, partial, sems,
):
    copies = [
        pltpu.make_async_copy(rows_hbm, src.at[pl.ds(0, TILES)], sems.at[0]),
        pltpu.make_async_copy(got1_hbm, src.at[pl.ds(TILES, CAP)], sems.at[1]),
        pltpu.make_async_copy(got2_hbm, src.at[pl.ds(TILES + CAP, CAP)], sems.at[2]),
    ]
    for copy in copies:
        copy.start()
    for copy in copies:
        copy.wait()
    diag = diag_ref[...]
    of_class = jnp.bitwise_and(iota((4 * NMAT, ROWS), 0), NMAT - 1)

    def own(kind, z):
        return own_ref[pl.ds(kind * PLANES + z, 1), :]

    def forward(z, before):
        for j in range(ROWS):
            dep[pl.ds(j, 1), :] = src[pl.ds(where_ref[z, j], 1), :]
        here = pl.ds(pl.multiple_of(z * ROWS, ROWS), ROWS)
        chosen = jnp.where(of_class == class_ref[pl.ds(z, 1), :], 1.0, 0.0).astype(jnp.bfloat16)
        weights = lax.dot_general(
            chosen, diag, (((0,), (0,)), ((), ())), preferred_element_type=jnp.float32
        )
        cells = dep[...]
        adv = (
            weights[:, :LANES] * cells
            + pltpu.roll(weights[:, LANES : 2 * LANES] * cells, 1, 1)
            + pltpu.roll(weights[:, 2 * LANES :] * cells, LANES - 1, 1)
        )
        a, b = 0.5 + adv, 2.0 + adv
        ab = a * b
        free = adv * ab / (ab + one_ref[here, :] * b + two_ref[here, :] * a)
        base_ref[here, :] = adv - free
        before = free * own(0, z) + before * own(1, z)
        partial[here, :] = before
        return before

    last = lax.fori_loop(0, PLANES, forward, jnp.zeros((ROWS, LANES), jnp.float32))

    def backward(k, after):
        z = PLANES - 1 - k
        here = pl.ds(pl.multiple_of(z * ROWS, ROWS), ROWS)
        after = partial[here, :] + after * own(2, z)
        base_ref[here, :] = base_ref[here, :] + after
        return after

    first = lax.fori_loop(0, PLANES, backward, jnp.zeros((ROWS, LANES), jnp.float32))
    share = ends_ref.shape[1] // 2
    for d in range(ends_ref.shape[0]):
        ends_ref[d, pl.ds(0, share), :] = first[d * share : (d + 1) * share, :]
        ends_ref[d, pl.ds(share, share), :] = last[d * share : (d + 1) * share, :]


def slab(where, rows, got1, got2, one, two, classes, diag, own, devices):
    return pl.pallas_call(
        slab_kernel,
        out_shape=(
            jax.ShapeDtypeStruct((TILES, LANES), jnp.float32),
            jax.ShapeDtypeStruct((devices, 2 * ROWS // devices, LANES), jnp.float32),
        ),
        in_specs=[pl.BlockSpec(memory_space=SMEM)]
        + [pl.BlockSpec(memory_space=pl.ANY)] * 3
        + [pl.BlockSpec(memory_space=VMEM)] * 5,
        out_specs=[pl.BlockSpec(memory_space=VMEM)] * 2,
        scratch_shapes=[
            pltpu.VMEM((TILES + 2 * CAP, LANES), jnp.float32),
            pltpu.VMEM((ROWS, LANES), jnp.float32),
            pltpu.VMEM((TILES, LANES), jnp.float32),
            pltpu.SemaphoreType.DMA((3,)),
        ],
        name="slab",
    )(where, rows, got1, got2, one, two, classes, diag, own)


def interface_kernel(ends_ref, red_ref, out_ref, carry_ref):
    devices, both, _ = ends_ref.shape
    share = both // 2
    coef = lambda kind, d: red_ref[kind, pl.ds(d, 1), :]
    upto = jnp.zeros((share, LANES), jnp.float32)
    for d in range(devices):
        first, last = ends_ref[d, pl.ds(0, share), :], ends_ref[d, pl.ds(share, share), :]
        carry_ref[d] = upto
        upto = last + coef(0, d) * first + coef(1, d) * upto
    after = jnp.zeros((share, LANES), jnp.float32)
    for d in range(devices - 1, -1, -1):
        first = ends_ref[d, pl.ds(0, share), :]
        out_ref[d, pl.ds(share, share), :] = after
        after = coef(2, d) * first + coef(3, d) * carry_ref[d] + coef(4, d) * after
        out_ref[d, pl.ds(0, share), :] = carry_ref[d] + coef(5, d) * after


def interface(ends, red):
    devices, both, _ = ends.shape
    return pl.pallas_call(
        interface_kernel,
        out_shape=jax.ShapeDtypeStruct(ends.shape, jnp.float32),
        in_specs=[pl.BlockSpec(memory_space=VMEM)] * 2,
        out_specs=pl.BlockSpec(memory_space=VMEM),
        scratch_shapes=[pltpu.VMEM((devices, both // 2, LANES), jnp.float32)],
        name="interface",
    )(ends, red)


def finish_kernel(base_ref, near_ref, own_ref, out_ref, left_t, right_t):
    devices, both, _ = near_ref.shape
    share = both // 2
    for d in range(devices):
        left_t[pl.ds(d * share, share), :] = near_ref[d, pl.ds(0, share), :]
        right_t[pl.ds(d * share, share), :] = near_ref[d, pl.ds(share, share), :]
    left, right = left_t[...], right_t[...]
    for z in range(PLANES):
        here = pl.ds(z * ROWS, ROWS)
        from_left = own_ref[pl.ds(3 * PLANES + z, 1), :]
        from_right = own_ref[pl.ds(4 * PLANES + z, 1), :]
        out_ref[here, :] = base_ref[here, :] + from_left * left + from_right * right


def finish(base, near, own):
    return pl.pallas_call(
        finish_kernel,
        out_shape=jax.ShapeDtypeStruct(base.shape, jnp.float32),
        in_specs=[pl.BlockSpec(memory_space=VMEM)] * 3,
        out_specs=pl.BlockSpec(memory_space=VMEM),
        scratch_shapes=[pltpu.VMEM((ROWS, LANES), jnp.float32)] * 2,
        name="finish",
    )(base, near, own)


def local(
    conc, target_one, target_two, diffusivity, src_shift, src_tile, interp_class, interp_mats
):
    devices = lax.axis_size("gy")
    rows = to_rows(conc)
    place = (src_tile & -64) | ((src_tile & 7) << 3) | ((src_tile >> 3) & 7)
    code = tile_order(src_shift * TILES + place)
    list1, list2, where = request(code)
    asked1, asked2 = shifted(list1, "gx", -1), shifted(list2, "gx", -2)
    face = 0.5 * (diffusivity[1:] + diffusivity[:-1])
    kl = jnp.pad(face, (1, 0)).reshape(devices, PLANES).T
    kr = jnp.pad(face, (0, 1)).reshape(devices, PLANES).T
    wide = ((0, 0), (0, LANES - devices))
    mine = (iota((1, LANES), 1) == lax.axis_index("gy")).astype(jnp.float32)
    own, red, diag = coefficients(jnp.pad(kl, wide), jnp.pad(kr, wide), mine, interp_mats, devices)
    send1, send2 = serve(asked1, asked2, rows)
    got1, got2 = shifted(send1, "gx", 1), shifted(send2, "gx", 2)
    base, ends = slab(
        where, rows, got1, got2, to_rows(target_one), to_rows(target_two),
        tile_order(interp_class), diag, own, devices,
    )
    ends = lax.all_to_all(ends, "gy", split_axis=0, concat_axis=0, tiled=True)
    near = interface(ends, red)
    near = lax.all_to_all(near, "gy", split_axis=0, concat_axis=0, tiled=True)
    return from_rows(finish(base, near, own), conc.shape)


def solution(mesh):
    slabs = P("gy", "gx", None)
    in_specs = (slabs, slabs, slabs, P(), slabs, slabs, slabs, P())
    return jax.shard_map(local, mesh=mesh, in_specs=in_specs, out_specs=slabs, check_vma=False)
```

```python
import jax
import jax.numpy as jnp
from jax import lax
from jax.experimental import pallas as pl
from jax.experimental.pallas import tpu as pltpu
from jax.sharding import PartitionSpec as P

LANES = 128
NMAT = 8
PLANES = 16
ROWS = 128
TILES = PLANES * ROWS
CAP = 512
HIGH = lax.Precision.HIGHEST
VMEM = pl.BlockSpec(memory_space=pltpu.VMEM)
SMEM = pl.BlockSpec(memory_space=pltpu.SMEM)
PARAMS = pltpu.CompilerParams(vmem_limit_bytes=24 << 20)


def near(value):
    return pltpu.with_memory_space_constraint(value, pltpu.VMEM)


def shifted(value, axis, by):
    peers = lax.axis_size(axis)
    pairs = [(i, i + by) for i in range(peers) if 0 <= i + by < peers]
    return lax.ppermute(value, axis, pairs)


def to_rows(value):
    z, x, y = value.shape
    value = value.reshape(z, x // 8, 8, y // LANES, LANES).transpose(0, 1, 3, 2, 4)
    return value.reshape(z * x * (y // LANES), LANES)


def from_rows(rows, shape):
    z, x, y = shape
    rows = rows.reshape(z, x // 8, y // LANES, 8, LANES).transpose(0, 1, 3, 2, 4)
    return rows.reshape(shape)


def iota(shape, axis):
    return lax.broadcasted_iota(jnp.int32, shape, axis)


def by_lanes(ref):
    return jnp.concatenate([ref[:, b, :] for b in range(ref.shape[1])], axis=1)


def ranks_of(mine):
    before_lane = (iota((LANES, LANES), 0) < iota((LANES, LANES), 1)).astype(jnp.bfloat16)
    before_row = (iota((PLANES, PLANES), 1) < iota((PLANES, PLANES), 0)).astype(jnp.bfloat16)
    all_lanes = jnp.ones((LANES, LANES), jnp.bfloat16)
    mask = jnp.where(mine, 1.0, 0.0).astype(jnp.bfloat16)
    inside = jnp.dot(mask, before_lane, preferred_element_type=jnp.float32)
    per_row = jnp.dot(mask, all_lanes, preferred_element_type=jnp.float32)
    ahead = jnp.dot(before_row, per_row.astype(jnp.bfloat16), preferred_element_type=jnp.float32)
    return jnp.where(mine, (inside + ahead).astype(jnp.int32), -1)


def compact(rank, value, empty, picked_ref):
    for block in range(CAP // 64):
        slot = iota((64, LANES), 0) + 64 * block
        picked = jnp.zeros((64, LANES), jnp.float32)
        for row in range(PLANES):
            picked = jnp.where(rank[row : row + 1, :] == slot, value[row : row + 1, :] - empty, picked)
        picked_ref[pl.ds(64 * block, 64), :] = picked
    total = lax.dot_general(
        jnp.ones((8, LANES), jnp.float32), picked_ref[...], (((1,), (1,)), ((), ())),
        precision=HIGH, preferred_element_type=jnp.float32,
    )
    return (total[0:1, :] + empty).astype(jnp.int32)


def request_kernel(shift_ref, tile_ref, list1_ref, list2_ref, place_ref, shift_out, picked_ref):
    shift, tile = by_lanes(shift_ref), by_lanes(tile_ref)
    place = (tile & -64) | ((tile & 7) << 3) | (lax.shift_right_logical(tile, 3) & 7)
    place_ref[...] = place
    shift_out[...] = shift
    place = place.astype(jnp.float32)
    for step, list_ref in ((1, list1_ref), (2, list2_ref)):
        list_ref[...] = compact(ranks_of(shift == step), place, 0.0, picked_ref)


def request(shift, tile):
    return pl.pallas_call(
        request_kernel,
        out_shape=(
            pltpu.VMEM((1, CAP), jnp.int32),
            pltpu.VMEM((1, CAP), jnp.int32),
            jax.ShapeDtypeStruct((PLANES, LANES), jnp.int32),
            pltpu.VMEM((PLANES, LANES), jnp.int32),
        ),
        in_specs=[VMEM] * 2,
        out_specs=[VMEM] * 4,
        scratch_shapes=[pltpu.VMEM((CAP, LANES), jnp.float32)],
        compiler_params=PARAMS,
        name="request",
    )(near(shift), near(tile))


def serve_kernel(list1_ref, list2_ref, rows_ref, out1_ref, out2_ref):
    for list_ref, out_ref in ((list1_ref, out1_ref), (list2_ref, out2_ref)):

        def step(k, carry, list_ref=list_ref, out_ref=out_ref):
            for j in range(32):
                slot = k * 32 + j
                out_ref[pl.ds(slot, 1), :] = rows_ref[pl.ds(list_ref[0, slot], 1), :]
            return carry

        lax.fori_loop(0, CAP // 32, step, 0)


def serve(list1, list2, rows):
    out = pltpu.VMEM((CAP, LANES), jnp.float32)
    return pl.pallas_call(
        serve_kernel,
        out_shape=(out, out),
        in_specs=[SMEM] * 2 + [VMEM],
        out_specs=[VMEM] * 2,
        compiler_params=PARAMS,
        name="serve",
    )(list1, list2, rows)


def coef_kernel(diff_ref, mats_ref, own_ref, red_ref, diag_ref, own_t, row_t):
    devices = red_ref.shape[1]
    row = lambda a, z: a[z : z + 1, :]
    lane = iota((1, LANES), 1)
    plane_of = (iota((PLANES, LANES), 1) & (PLANES - 1)) == iota((PLANES, LANES), 0)
    diff = jnp.zeros((PLANES, LANES), jnp.float32)
    per_row = LANES // PLANES
    for r in range(diff_ref.shape[0]):
        goes = iota((LANES, LANES), 1) == lax.shift_right_logical(iota((LANES, LANES), 0), 4) + per_row * r
        diff = diff + jnp.dot(
            jnp.where(plane_of, diff_ref[pl.ds(r, 1), :], 0.0), jnp.where(goes, 1.0, 0.0),
            precision=HIGH, preferred_element_type=jnp.float32,
        )
    kr = [0.5 * (row(diff, z + 1) + row(diff, z)) for z in range(PLANES - 1)]
    beyond = pltpu.roll(diff, LANES - 1, 1)
    kr.append(jnp.where(lane < devices - 1, 0.5 * (row(beyond, 0) + row(diff, PLANES - 1)), 0.0))
    kl = [jnp.where(lane > 0, pltpu.roll(jnp.broadcast_to(kr[-1], (8, LANES)), 1, 1)[0:1, :], 0.0)]
    kl = kl + kr[:-1]
    inv, low, up = [], [], []
    for z in range(PLANES):
        pivot = 1.0 + kl[z] + kr[z]
        if z > 0:
            pivot = pivot - kr[z - 1] * up[z - 1]
        inv.append(1.0 / pivot)
        low.append(jnp.zeros_like(pivot) if z == 0 else kr[z - 1] * inv[z])
        up.append(kr[z] * inv[z])
    left = [kl[0] * inv[0]]
    for z in range(1, PLANES):
        left.append(low[z] * left[z - 1])
    right = [None] * PLANES
    right[-1] = up[-1]
    for z in range(PLANES - 2, -1, -1):
        left[z] = left[z] + up[z] * left[z + 1]
        right[z] = up[z] * right[z + 1]
    mine = lane == lax.axis_index("gy")
    ones = jnp.ones((LANES, LANES), jnp.float32)
    for kind, values in enumerate((inv, low, up, left, right)):
        for z in range(PLANES):
            own_t[pl.ds(kind * PLANES + z, 1), :] = jnp.where(mine, values[z], 0.0)
    own_ref[...] = jnp.dot(own_t[...], ones, precision=HIGH, preferred_element_type=jnp.float32)
    eye = iota((devices, LANES), 0) == iota((devices, LANES), 1)
    for kind, value in enumerate((left[0], left[-1], right[0], right[-1])):
        row_t[pl.ds(kind * devices, devices), :] = jnp.where(eye, value, 0.0)
    spread = jnp.dot(row_t[...], ones, precision=HIGH, preferred_element_type=jnp.float32)
    ratio = jnp.zeros((1, LANES), jnp.float32)
    for d in range(devices):
        l_first, l_last, r_first, r_last = (row(spread, kind * devices + d) for kind in range(4))
        gain = 1.0 / (1.0 - l_first * ratio)
        for kind, value in enumerate(
            (l_last * ratio * gain, l_last * gain, gain, gain * l_first, gain * r_first, ratio)
        ):
            red_ref[kind, pl.ds(d, 1), :] = value
        ratio = r_last + l_last * ratio * gain * r_first
    r, c = iota((LANES, LANES), 0), iota((LANES, LANES), 1)
    for kind, at in enumerate((r == c, r == c + 1, r == c - 1)):
        values = jnp.concatenate(
            [jnp.sum(jnp.where(at, mats_ref[m], 0.0), axis=0, keepdims=True) for m in range(NMAT)], axis=0
        )
        first = values.astype(jnp.bfloat16).astype(jnp.float32)
        second = (values - first).astype(jnp.bfloat16).astype(jnp.float32)
        third = values - first - second
        stacked = jnp.concatenate([first, second, third, jnp.zeros_like(first)], axis=0)
        diag_ref[:, pl.ds(kind * LANES, LANES)] = stacked.astype(jnp.bfloat16)


def coefficients(diffusivity, mats, devices):
    return pl.pallas_call(
        coef_kernel,
        out_shape=(
            pltpu.VMEM((5 * PLANES, LANES), jnp.float32),
            pltpu.VMEM((6, devices, LANES), jnp.float32),
            pltpu.VMEM((4 * NMAT, 3 * LANES), jnp.bfloat16),
        ),
        in_specs=[VMEM] * 2,
        out_specs=[VMEM] * 3,
        scratch_shapes=[
            pltpu.VMEM((5 * PLANES, LANES), jnp.float32),
            pltpu.VMEM((4 * devices, LANES), jnp.float32),
        ],
        compiler_params=PARAMS,
        cost_estimate=pl.CostEstimate(flops=8_000_000, bytes_accessed=4_000_000, transcendentals=0),
        name="coefficients",
    )(diffusivity.reshape(-1, LANES), near(mats))


def local_kernel(
    place_ref, rows_ref, shift_ref, class_ref, diag_ref, dep_ref, weights_ref, to1_ref, to2_ref, picked_ref
):
    shift = shift_ref[...]
    spot = iota((PLANES, LANES), 1)
    spot = ((spot & 8) << 3) | (lax.shift_right_logical(spot, 4) << 3) | (spot & 7)
    spot = (spot + ROWS * iota((PLANES, LANES), 0)).astype(jnp.float32)
    for step, to_ref in ((1, to1_ref), (2, to2_ref)):
        to_ref[...] = compact(ranks_of(shift == step), spot, float(TILES), picked_ref)
    classes = by_lanes(class_ref)
    diag = diag_ref[...]
    of_class = jnp.bitwise_and(iota((4 * NMAT, ROWS), 0), NMAT - 1)
    for z in range(PLANES):
        chosen = jnp.where(of_class == classes[z : z + 1, :], 1.0, 0.0).astype(jnp.bfloat16)
        weights = lax.dot_general(
            chosen, diag, (((0,), (0,)), ((), ())), preferred_element_type=jnp.float32
        )
        for group in range(ROWS // 8):
            at = z * ROWS + (group % 2) * 64 + (group // 2) * 8
            weights_ref[pl.ds(at, 8), :] = weights[group * 8 : group * 8 + 8, :]

    def plane(z, carry):
        start = pl.multiple_of(z * ROWS, ROWS)
        for j in range(ROWS):
            at = ((j >> 3) & 1) * 64 + (j >> 4) * 8 + (j & 7)
            dep_ref[pl.ds(start + at, 1), :] = rows_ref[pl.ds(place_ref[z, j], 1), :]
        return carry

    lax.fori_loop(0, PLANES, plane, 0)


def before_arrival(place, rows, shift, classes, diag):
    return pl.pallas_call(
        local_kernel,
        out_shape=(
            pltpu.VMEM((TILES + 8, LANES), jnp.float32),
            pltpu.VMEM((TILES, 3 * LANES), jnp.float32),
            jax.ShapeDtypeStruct((1, CAP), jnp.int32),
            jax.ShapeDtypeStruct((1, CAP), jnp.int32),
        ),
        in_specs=[SMEM] + [VMEM] * 4,
        out_specs=[VMEM] * 4,
        scratch_shapes=[pltpu.VMEM((CAP, LANES), jnp.float32)],
        compiler_params=PARAMS,
        cost_estimate=pl.CostEstimate(flops=20_000_000, bytes_accessed=10_000_000, transcendentals=0),
        name="before_arrival",
    )(place, rows, near(shift), near(classes), near(diag))


def slab_kernel(
    to1_ref, to2_ref, got1_ref, got2_ref, dep_in, weights_ref, one_ref, two_ref, own_ref,
    base_ref, ends_ref, dep_ref, partial,
):
    del dep_in
    for to_ref, got_ref in ((to1_ref, got1_ref), (to2_ref, got2_ref)):

        def patch(k, carry, to_ref=to_ref, got_ref=got_ref):
            start = pl.multiple_of(k * 32, 32)
            for j in range(32):
                dep_ref[pl.ds(to_ref[0, start + j], 1), :] = got_ref[pl.ds(start + j, 1), :]
            return carry

        lax.fori_loop(0, CAP // 32, patch, 0)

    def own(kind, z):
        return own_ref[pl.ds(kind * PLANES + z, 1), :]

    def forward(z, before):
        here = pl.ds(pl.multiple_of(z * ROWS, ROWS), ROWS)
        cells = dep_ref[here, :]
        adv = (
            weights_ref[here, pl.ds(0, LANES)] * cells
            + pltpu.roll(weights_ref[here, pl.ds(LANES, LANES)] * cells, 1, 1)
            + pltpu.roll(weights_ref[here, pl.ds(2 * LANES, LANES)] * cells, LANES - 1, 1)
        )
        a, b = 0.5 + adv, 2.0 + adv
        ab = a * b
        free = adv * ab / (ab + one_ref[here, :] * b + two_ref[here, :] * a)
        base_ref[here, :] = adv - free
        before = free * own(0, z) + before * own(1, z)
        partial[here, :] = before
        return before

    last = lax.fori_loop(0, PLANES, forward, jnp.zeros((ROWS, LANES), jnp.float32))

    def backward(k, after):
        z = PLANES - 1 - k
        here = pl.ds(pl.multiple_of(z * ROWS, ROWS), ROWS)
        after = partial[here, :] + after * own(2, z)
        base_ref[here, :] = base_ref[here, :] + after
        return after

    first = lax.fori_loop(0, PLANES, backward, jnp.zeros((ROWS, LANES), jnp.float32))
    share = ends_ref.shape[1] // 2
    for d in range(ends_ref.shape[0]):
        ends_ref[d, pl.ds(0, share), :] = first[d * share : (d + 1) * share, :]
        ends_ref[d, pl.ds(share, share), :] = last[d * share : (d + 1) * share, :]


def slab(to1, to2, got1, got2, dep, weights, one, two, own, devices):
    base, ends, _ = pl.pallas_call(
        slab_kernel,
        out_shape=(
            pltpu.VMEM((TILES, LANES), jnp.float32),
            pltpu.VMEM((devices, 2 * ROWS // devices, LANES), jnp.float32),
            pltpu.VMEM((TILES + 8, LANES), jnp.float32),
        ),
        in_specs=[SMEM] * 2 + [VMEM] * 7,
        out_specs=[VMEM] * 3,
        scratch_shapes=[pltpu.VMEM((TILES, LANES), jnp.float32)],
        input_output_aliases={4: 2},
        compiler_params=PARAMS,
        name="slab",
    )(to1, to2, near(got1), near(got2), near(dep), near(weights), near(one), near(two), near(own))
    return base, ends


def interface_kernel(ends_ref, red_ref, out_ref, carry_ref):
    devices, both, _ = ends_ref.shape
    share = both // 2
    coef = lambda kind, d: red_ref[kind, pl.ds(d, 1), :]
    upto = jnp.zeros((share, LANES), jnp.float32)
    for d in range(devices):
        first, last = ends_ref[d, pl.ds(0, share), :], ends_ref[d, pl.ds(share, share), :]
        carry_ref[d] = upto
        upto = last + coef(0, d) * first + coef(1, d) * upto
    after = jnp.zeros((share, LANES), jnp.float32)
    for d in range(devices - 1, -1, -1):
        first = ends_ref[d, pl.ds(0, share), :]
        out_ref[d, pl.ds(share, share), :] = after
        after = coef(2, d) * first + coef(3, d) * carry_ref[d] + coef(4, d) * after
        out_ref[d, pl.ds(0, share), :] = carry_ref[d] + coef(5, d) * after


def interface(ends, red):
    devices, both, _ = ends.shape
    return pl.pallas_call(
        interface_kernel,
        out_shape=pltpu.VMEM(ends.shape, jnp.float32),
        in_specs=[VMEM] * 2,
        out_specs=VMEM,
        scratch_shapes=[pltpu.VMEM((devices, both // 2, LANES), jnp.float32)],
        compiler_params=PARAMS,
        name="interface",
    )(near(ends), near(red))


def finish_kernel(base_ref, near_ref, own_ref, out_ref, left_t, right_t):
    devices, both, _ = near_ref.shape
    share = both // 2
    for d in range(devices):
        left_t[pl.ds(d * share, share), :] = near_ref[d, pl.ds(0, share), :]
        right_t[pl.ds(d * share, share), :] = near_ref[d, pl.ds(share, share), :]
    left, right = left_t[...], right_t[...]
    for z in range(PLANES):
        here = pl.ds(z * ROWS, ROWS)
        from_left = own_ref[pl.ds(3 * PLANES + z, 1), :]
        from_right = own_ref[pl.ds(4 * PLANES + z, 1), :]
        out_ref[here, :] = base_ref[here, :] + from_left * left + from_right * right


def finish(base, sides, own):
    return pl.pallas_call(
        finish_kernel,
        out_shape=jax.ShapeDtypeStruct(base.shape, jnp.float32),
        in_specs=[VMEM] * 3,
        out_specs=VMEM,
        scratch_shapes=[pltpu.VMEM((ROWS, LANES), jnp.float32)] * 2,
        compiler_params=PARAMS,
        name="finish",
    )(near(base), near(sides), near(own))


def local(
    conc, target_one, target_two, diffusivity, src_shift, src_tile, interp_class, interp_mats
):
    devices = lax.axis_size("gy")
    rows = near(to_rows(conc))
    as_stored = lambda value: value.transpose(0, 2, 1)
    list1, list2, place, shift = request(as_stored(src_shift), as_stored(src_tile))
    asked1, asked2 = shifted(list1, "gx", -1), shifted(list2, "gx", -2)
    own, red, diag = coefficients(diffusivity, interp_mats, devices)
    send1, send2 = serve(asked1, asked2, rows)
    got1, got2 = shifted(send1, "gx", 1), shifted(send2, "gx", 2)
    dep, weights, to1, to2 = before_arrival(place, rows, shift, as_stored(interp_class), diag)
    base, ends = slab(
        to1, to2, got1, got2, dep, weights, to_rows(target_one), to_rows(target_two), own, devices
    )
    ends = lax.all_to_all(ends, "gy", split_axis=0, concat_axis=0, tiled=True)
    sides = interface(ends, red)
    sides = lax.all_to_all(sides, "gy", split_axis=0, concat_axis=0, tiled=True)
    return from_rows(finish(base, sides, own), conc.shape)


def solution(mesh):
    slabs = P("gy", "gx", None)
    in_specs = (slabs, slabs, slabs, P(), slabs, slabs, slabs, P())
    return jax.shard_map(local, mesh=mesh, in_specs=in_specs, out_specs=slabs, check_vma=False)
```

```python
import jax
import jax.numpy as jnp
from jax import lax
from jax.experimental import pallas as pl
from jax.experimental.pallas import tpu as pltpu
from jax.sharding import PartitionSpec as P

LANES = 128
NMAT = 8
PLANES = 16
ROWS = 128
TILES = PLANES * ROWS
CAP = 512
HIGH = lax.Precision.HIGHEST
VMEM = pl.BlockSpec(memory_space=pltpu.VMEM)
SMEM = pl.BlockSpec(memory_space=pltpu.SMEM)
ANY = pl.BlockSpec(memory_space=pl.ANY)
PARAMS = pltpu.CompilerParams(vmem_limit_bytes=24 << 20)


def near(value):
    return pltpu.with_memory_space_constraint(value, pltpu.VMEM)


def shifted(value, axis, by):
    peers = lax.axis_size(axis)
    pairs = [(i, i + by) for i in range(peers) if 0 <= i + by < peers]
    return lax.ppermute(value, axis, pairs)


def far(value):
    return pltpu.with_memory_space_constraint(value, pltpu.HBM)


def to_rows(value):
    z, x, y = value.shape
    value = value.reshape(z, x // 8, 8, y // LANES, LANES).transpose(0, 1, 3, 2, 4)
    return value.reshape(z * x * (y // LANES), LANES)


def from_rows(rows, shape):
    z, x, y = shape
    rows = rows.reshape(z, x // 8, y // LANES, 8, LANES).transpose(0, 1, 3, 2, 4)
    return rows.reshape(shape)


def iota(shape, axis):
    return lax.broadcasted_iota(jnp.int32, shape, axis)


def by_lanes(ref):
    return jnp.concatenate([ref[:, b, :] for b in range(ref.shape[1])], axis=1)


def ranks_of(mine):
    before_lane = (iota((LANES, LANES), 0) < iota((LANES, LANES), 1)).astype(jnp.bfloat16)
    before_row = (iota((PLANES, PLANES), 1) < iota((PLANES, PLANES), 0)).astype(jnp.bfloat16)
    all_lanes = jnp.ones((LANES, LANES), jnp.bfloat16)
    mask = jnp.where(mine, 1.0, 0.0).astype(jnp.bfloat16)
    inside = jnp.dot(mask, before_lane, preferred_element_type=jnp.float32)
    per_row = jnp.dot(mask, all_lanes, preferred_element_type=jnp.float32)
    ahead = jnp.dot(before_row, per_row.astype(jnp.bfloat16), preferred_element_type=jnp.float32)
    return jnp.where(mine, (inside + ahead).astype(jnp.int32), -1)


def compact(rank, value, empty, picked_ref):
    for block in range(CAP // 64):
        slot = iota((64, LANES), 0) + 64 * block
        picked = jnp.zeros((64, LANES), jnp.float32)
        for row in range(PLANES):
            picked = jnp.where(rank[row : row + 1, :] == slot, value[row : row + 1, :] - empty, picked)
        picked_ref[pl.ds(64 * block, 64), :] = picked
    total = lax.dot_general(
        jnp.ones((8, LANES), jnp.float32), picked_ref[...], (((1,), (1,)), ((), ())),
        precision=HIGH, preferred_element_type=jnp.float32,
    )
    return (total[0:1, :] + empty).astype(jnp.int32)


def request_kernel(
    shift_ref, tile_ref, rows_hbm, list1_ref, list2_ref, place_ref, shift_out, rows_ref, picked_ref, sem
):
    copy = pltpu.make_async_copy(rows_hbm, rows_ref, sem)
    copy.start()
    shift, tile = by_lanes(shift_ref), by_lanes(tile_ref)
    place = (tile & -64) | ((tile & 7) << 3) | (lax.shift_right_logical(tile, 3) & 7)
    place_ref[...] = place
    shift_out[...] = shift
    place = place.astype(jnp.float32)
    for step, list_ref in ((1, list1_ref), (2, list2_ref)):
        list_ref[...] = compact(ranks_of(shift == step), place, 0.0, picked_ref)
    copy.wait()


def request(shift, tile, rows):
    return pl.pallas_call(
        request_kernel,
        out_shape=(
            pltpu.VMEM((1, CAP), jnp.int32),
            pltpu.VMEM((1, CAP), jnp.int32),
            jax.ShapeDtypeStruct((PLANES, LANES), jnp.int32),
            pltpu.VMEM((PLANES, LANES), jnp.int32),
            pltpu.VMEM((TILES, LANES), jnp.float32),
        ),
        in_specs=[VMEM] * 2 + [ANY],
        out_specs=[VMEM] * 5,
        scratch_shapes=[pltpu.VMEM((CAP, LANES), jnp.float32), pltpu.SemaphoreType.DMA],
        compiler_params=PARAMS,
        name="request",
    )(far(shift), far(tile), far(rows))


def serve_kernel(list_ref, rows_ref, out_ref):
    def step(k, carry):
        for j in range(32):
            slot = k * 32 + j
            out_ref[pl.ds(slot, 1), :] = rows_ref[pl.ds(list_ref[0, slot], 1), :]
        return carry

    lax.fori_loop(0, CAP // 32, step, 0)


def serve(wanted, rows):
    return pl.pallas_call(
        serve_kernel,
        out_shape=pltpu.VMEM((CAP, LANES), jnp.float32),
        in_specs=[SMEM, VMEM],
        out_specs=VMEM,
        compiler_params=PARAMS,
        name="serve",
    )(wanted, near(rows))


def coef_kernel(diff_ref, mats_ref, own_ref, red_ref, diag_ref, own_t, row_t):
    devices = red_ref.shape[1]
    row = lambda a, z: a[z : z + 1, :]
    lane = iota((1, LANES), 1)
    plane_of = (iota((PLANES, LANES), 1) & (PLANES - 1)) == iota((PLANES, LANES), 0)
    diff = jnp.zeros((PLANES, LANES), jnp.float32)
    per_row = LANES // PLANES
    for r in range(diff_ref.shape[0]):
        goes = iota((LANES, LANES), 1) == lax.shift_right_logical(iota((LANES, LANES), 0), 4) + per_row * r
        diff = diff + jnp.dot(
            jnp.where(plane_of, diff_ref[pl.ds(r, 1), :], 0.0), jnp.where(goes, 1.0, 0.0),
            precision=HIGH, preferred_element_type=jnp.float32,
        )
    kr = [0.5 * (row(diff, z + 1) + row(diff, z)) for z in range(PLANES - 1)]
    beyond = pltpu.roll(diff, LANES - 1, 1)
    kr.append(jnp.where(lane < devices - 1, 0.5 * (row(beyond, 0) + row(diff, PLANES - 1)), 0.0))
    kl = [jnp.where(lane > 0, pltpu.roll(jnp.broadcast_to(kr[-1], (8, LANES)), 1, 1)[0:1, :], 0.0)]
    kl = kl + kr[:-1]
    inv, low, up = [], [], []
    for z in range(PLANES):
        pivot = 1.0 + kl[z] + kr[z]
        if z > 0:
            pivot = pivot - kr[z - 1] * up[z - 1]
        inv.append(1.0 / pivot)
        low.append(jnp.zeros_like(pivot) if z == 0 else kr[z - 1] * inv[z])
        up.append(kr[z] * inv[z])
    left = [kl[0] * inv[0]]
    for z in range(1, PLANES):
        left.append(low[z] * left[z - 1])
    right = [None] * PLANES
    right[-1] = up[-1]
    for z in range(PLANES - 2, -1, -1):
        left[z] = left[z] + up[z] * left[z + 1]
        right[z] = up[z] * right[z + 1]
    mine = lane == lax.axis_index("gy")
    ones = jnp.ones((LANES, LANES), jnp.float32)
    for kind, values in enumerate((inv, low, up, left, right)):
        for z in range(PLANES):
            own_t[pl.ds(kind * PLANES + z, 1), :] = jnp.where(mine, values[z], 0.0)
    own_ref[...] = jnp.dot(own_t[...], ones, precision=HIGH, preferred_element_type=jnp.float32)
    eye = iota((devices, LANES), 0) == iota((devices, LANES), 1)
    for kind, value in enumerate((left[0], left[-1], right[0], right[-1])):
        row_t[pl.ds(kind * devices, devices), :] = jnp.where(eye, value, 0.0)
    spread = jnp.dot(row_t[...], ones, precision=HIGH, preferred_element_type=jnp.float32)
    ratio = jnp.zeros((1, LANES), jnp.float32)
    for d in range(devices):
        l_first, l_last, r_first, r_last = (row(spread, kind * devices + d) for kind in range(4))
        gain = 1.0 / (1.0 - l_first * ratio)
        for kind, value in enumerate(
            (l_last * ratio * gain, l_last * gain, gain, gain * l_first, gain * r_first, ratio)
        ):
            red_ref[kind, pl.ds(d, 1), :] = value
        ratio = r_last + l_last * ratio * gain * r_first
    r, c = iota((LANES, LANES), 0), iota((LANES, LANES), 1)
    for kind, at in enumerate((r == c, r == c + 1, r == c - 1)):
        values = jnp.concatenate(
            [jnp.sum(jnp.where(at, mats_ref[m], 0.0), axis=0, keepdims=True) for m in range(NMAT)], axis=0
        )
        first = values.astype(jnp.bfloat16).astype(jnp.float32)
        second = (values - first).astype(jnp.bfloat16).astype(jnp.float32)
        third = values - first - second
        stacked = jnp.concatenate([first, second, third, jnp.zeros_like(first)], axis=0)
        diag_ref[:, pl.ds(kind * LANES, LANES)] = stacked.astype(jnp.bfloat16)


def coefficients(diffusivity, mats, devices):
    return pl.pallas_call(
        coef_kernel,
        out_shape=(
            pltpu.VMEM((5 * PLANES, LANES), jnp.float32),
            pltpu.VMEM((6, devices, LANES), jnp.float32),
            pltpu.VMEM((4 * NMAT, 3 * LANES), jnp.bfloat16),
        ),
        in_specs=[VMEM] * 2,
        out_specs=[VMEM] * 3,
        scratch_shapes=[
            pltpu.VMEM((5 * PLANES, LANES), jnp.float32),
            pltpu.VMEM((4 * devices, LANES), jnp.float32),
        ],
        compiler_params=PARAMS,
        cost_estimate=pl.CostEstimate(flops=8_000_000, bytes_accessed=4_000_000, transcendentals=0),
        name="coefficients",
    )(diffusivity.reshape(-1, LANES), mats)


def local_kernel(
    place_ref, rows_ref, shift_ref, class_ref, diag_ref, one_hbm, two_hbm,
    dep_ref, weights_ref, to1_ref, to2_ref, one_ref, two_ref, picked_ref, sems,
):
    copies = [
        pltpu.make_async_copy(one_hbm, one_ref, sems.at[0]),
        pltpu.make_async_copy(two_hbm, two_ref, sems.at[1]),
    ]
    for copy in copies:
        copy.start()
    shift = shift_ref[...]
    spot = iota((PLANES, LANES), 1)
    spot = ((spot & 8) << 3) | (lax.shift_right_logical(spot, 4) << 3) | (spot & 7)
    spot = (spot + ROWS * iota((PLANES, LANES), 0)).astype(jnp.float32)
    for step, to_ref in ((1, to1_ref), (2, to2_ref)):
        to_ref[...] = compact(ranks_of(shift == step), spot, float(TILES), picked_ref)
    classes = by_lanes(class_ref)
    diag = diag_ref[...]
    of_class = jnp.bitwise_and(iota((4 * NMAT, ROWS), 0), NMAT - 1)
    for z in range(PLANES):
        chosen = jnp.where(of_class == classes[z : z + 1, :], 1.0, 0.0).astype(jnp.bfloat16)
        weights = lax.dot_general(
            chosen, diag, (((0,), (0,)), ((), ())), preferred_element_type=jnp.float32
        )
        for group in range(ROWS // 8):
            at = z * ROWS + (group % 2) * 64 + (group // 2) * 8
            weights_ref[pl.ds(at, 8), :] = weights[group * 8 : group * 8 + 8, :]

    def plane(z, carry):
        start = pl.multiple_of(z * ROWS, ROWS)
        for j in range(ROWS):
            at = ((j >> 3) & 1) * 64 + (j >> 4) * 8 + (j & 7)
            dep_ref[pl.ds(start + at, 1), :] = rows_ref[pl.ds(place_ref[z, j], 1), :]
        return carry

    lax.fori_loop(0, PLANES, plane, 0)
    for copy in copies:
        copy.wait()


def before_arrival(place, rows, shift, classes, diag, one, two):
    return pl.pallas_call(
        local_kernel,
        out_shape=(
            pltpu.VMEM((TILES + 8, LANES), jnp.float32),
            pltpu.VMEM((TILES, 3 * LANES), jnp.float32),
            jax.ShapeDtypeStruct((1, CAP), jnp.int32),
            jax.ShapeDtypeStruct((1, CAP), jnp.int32),
            pltpu.VMEM((TILES, LANES), jnp.float32),
            pltpu.VMEM((TILES, LANES), jnp.float32),
        ),
        in_specs=[SMEM] + [VMEM] * 4 + [ANY] * 2,
        out_specs=[VMEM] * 6,
        scratch_shapes=[pltpu.VMEM((CAP, LANES), jnp.float32), pltpu.SemaphoreType.DMA((2,))],
        compiler_params=PARAMS,
        cost_estimate=pl.CostEstimate(flops=20_000_000, bytes_accessed=10_000_000, transcendentals=0),
        name="before_arrival",
    )(place, near(rows), near(shift), classes, near(diag), far(one), far(two))


def patch_kernel(to_ref, got_ref, dep_in, dep_ref):
    del dep_in

    def patch(k, carry):
        start = pl.multiple_of(k * 32, 32)
        for j in range(32):
            dep_ref[pl.ds(to_ref[0, start + j], 1), :] = got_ref[pl.ds(start + j, 1), :]
        return carry

    lax.fori_loop(0, CAP // 32, patch, 0)


def patched(to, got, dep):
    return pl.pallas_call(
        patch_kernel,
        out_shape=pltpu.VMEM(dep.shape, jnp.float32),
        in_specs=[SMEM] + [VMEM] * 2,
        out_specs=VMEM,
        input_output_aliases={2: 0},
        compiler_params=PARAMS,
        name="patch",
    )(to, near(got), near(dep))


def slab_kernel(
    to_ref, got_ref, dep_in, weights_ref, one_ref, two_ref, own_ref, base_ref, ends_ref, dep_ref, partial
):
    patch_kernel(to_ref, got_ref, dep_in, dep_ref)

    def own(kind, z):
        return own_ref[pl.ds(kind * PLANES + z, 1), :]

    def forward(z, before):
        here = pl.ds(pl.multiple_of(z * ROWS, ROWS), ROWS)
        cells = dep_ref[here, :]
        adv = (
            weights_ref[here, pl.ds(0, LANES)] * cells
            + pltpu.roll(weights_ref[here, pl.ds(LANES, LANES)] * cells, 1, 1)
            + pltpu.roll(weights_ref[here, pl.ds(2 * LANES, LANES)] * cells, LANES - 1, 1)
        )
        a, b = 0.5 + adv, 2.0 + adv
        ab = a * b
        free = adv * ab / (ab + one_ref[here, :] * b + two_ref[here, :] * a)
        base_ref[here, :] = adv - free
        before = free * own(0, z) + before * own(1, z)
        partial[here, :] = before
        return before

    last = lax.fori_loop(0, PLANES, forward, jnp.zeros((ROWS, LANES), jnp.float32))

    def backward(k, after):
        z = PLANES - 1 - k
        here = pl.ds(pl.multiple_of(z * ROWS, ROWS), ROWS)
        after = partial[here, :] + after * own(2, z)
        base_ref[here, :] = base_ref[here, :] + after
        return after

    first = lax.fori_loop(0, PLANES, backward, jnp.zeros((ROWS, LANES), jnp.float32))
    share = ends_ref.shape[1] // 2
    for d in range(ends_ref.shape[0]):
        ends_ref[d, pl.ds(0, share), :] = first[d * share : (d + 1) * share, :]
        ends_ref[d, pl.ds(share, share), :] = last[d * share : (d + 1) * share, :]


def slab(to, got, dep, weights, one, two, own, devices):
    base, ends, _ = pl.pallas_call(
        slab_kernel,
        out_shape=(
            pltpu.VMEM((TILES, LANES), jnp.float32),
            pltpu.VMEM((devices, 2 * ROWS // devices, LANES), jnp.float32),
            pltpu.VMEM((TILES + 8, LANES), jnp.float32),
        ),
        in_specs=[SMEM] + [VMEM] * 6,
        out_specs=[VMEM] * 3,
        scratch_shapes=[pltpu.VMEM((TILES, LANES), jnp.float32)],
        input_output_aliases={2: 2},
        compiler_params=PARAMS,
        name="slab",
    )(to, near(got), near(dep), near(weights), near(one), near(two), near(own))
    return base, ends


def interface_kernel(ends_ref, red_ref, out_ref, carry_ref):
    devices, both, _ = ends_ref.shape
    share = both // 2
    coef = lambda kind, d: red_ref[kind, pl.ds(d, 1), :]
    upto = jnp.zeros((share, LANES), jnp.float32)
    for d in range(devices):
        first, last = ends_ref[d, pl.ds(0, share), :], ends_ref[d, pl.ds(share, share), :]
        carry_ref[d] = upto
        upto = last + coef(0, d) * first + coef(1, d) * upto
    after = jnp.zeros((share, LANES), jnp.float32)
    for d in range(devices - 1, -1, -1):
        first = ends_ref[d, pl.ds(0, share), :]
        out_ref[d, pl.ds(share, share), :] = after
        after = coef(2, d) * first + coef(3, d) * carry_ref[d] + coef(4, d) * after
        out_ref[d, pl.ds(0, share), :] = carry_ref[d] + coef(5, d) * after


def interface(ends, red):
    devices, both, _ = ends.shape
    return pl.pallas_call(
        interface_kernel,
        out_shape=pltpu.VMEM(ends.shape, jnp.float32),
        in_specs=[VMEM] * 2,
        out_specs=VMEM,
        scratch_shapes=[pltpu.VMEM((devices, both // 2, LANES), jnp.float32)],
        compiler_params=PARAMS,
        name="interface",
    )(near(ends), near(red))


def finish_kernel(base_ref, near_ref, own_ref, out_ref, left_t, right_t):
    devices, both, _ = near_ref.shape
    share = both // 2
    for d in range(devices):
        left_t[pl.ds(d * share, share), :] = near_ref[d, pl.ds(0, share), :]
        right_t[pl.ds(d * share, share), :] = near_ref[d, pl.ds(share, share), :]
    left, right = left_t[...], right_t[...]
    for z in range(PLANES):
        here = pl.ds(z * ROWS, ROWS)
        from_left = own_ref[pl.ds(3 * PLANES + z, 1), :]
        from_right = own_ref[pl.ds(4 * PLANES + z, 1), :]
        out_ref[here, :] = base_ref[here, :] + from_left * left + from_right * right


def finish(base, sides, own):
    return pl.pallas_call(
        finish_kernel,
        out_shape=jax.ShapeDtypeStruct(base.shape, jnp.float32),
        in_specs=[VMEM] * 3,
        out_specs=VMEM,
        scratch_shapes=[pltpu.VMEM((ROWS, LANES), jnp.float32)] * 2,
        compiler_params=PARAMS,
        name="finish",
    )(near(base), near(sides), near(own))


def local(
    conc, target_one, target_two, diffusivity, src_shift, src_tile, interp_class, interp_mats
):
    devices = lax.axis_size("gy")
    as_stored = lambda value: value.transpose(0, 2, 1)
    list1, list2, place, shift, rows = request(as_stored(src_shift), as_stored(src_tile), to_rows(conc))
    asked2, asked1 = shifted(list2, "gx", -2), shifted(list1, "gx", -1)
    own, red, diag = coefficients(diffusivity, interp_mats, devices)
    got2 = shifted(serve(asked2, rows), "gx", 2)
    got1 = shifted(serve(asked1, rows), "gx", 1)
    dep, weights, to1, to2, one, two = before_arrival(
        place, rows, shift, as_stored(interp_class), diag, to_rows(target_one), to_rows(target_two)
    )
    dep = patched(to1, got1, dep)
    base, ends = slab(to2, got2, dep, weights, one, two, own, devices)
    ends = lax.all_to_all(ends, "gy", split_axis=0, concat_axis=0, tiled=True)
    sides = interface(ends, red)
    sides = lax.all_to_all(sides, "gy", split_axis=0, concat_axis=0, tiled=True)
    return from_rows(finish(base, sides, own), conc.shape)


def solution(mesh):
    slabs = P("gy", "gx", None)
    in_specs = (slabs, slabs, slabs, P(), slabs, slabs, slabs, P())
    return jax.shard_map(local, mesh=mesh, in_specs=in_specs, out_specs=slabs, check_vma=False)
```

```python
import jax
import jax.numpy as jnp
from jax import lax
from jax.experimental import pallas as pl
from jax.experimental.pallas import tpu as pltpu
from jax.sharding import PartitionSpec as P

LANES = 128
NMAT = 8
PLANES = 16
ROWS = 128
TILES = PLANES * ROWS
CAP = 512
GROUP = 8
HIGH = lax.Precision.HIGHEST
VMEM = pl.BlockSpec(memory_space=pltpu.VMEM)
SMEM = pl.BlockSpec(memory_space=pltpu.SMEM)
ANY = pl.BlockSpec(memory_space=pl.ANY)
PARAMS = pltpu.CompilerParams(vmem_limit_bytes=24 << 20)


def near(value):
    return pltpu.with_memory_space_constraint(value, pltpu.VMEM)


def shifted(value, axis, by):
    peers = lax.axis_size(axis)
    pairs = [(i, i + by) for i in range(peers) if 0 <= i + by < peers]
    return lax.ppermute(value, axis, pairs)


def far(value):
    return pltpu.with_memory_space_constraint(value, pltpu.HBM)


def to_rows(value):
    z, x, y = value.shape
    value = value.reshape(z, x // 8, 8, y // LANES, LANES).transpose(0, 1, 3, 2, 4)
    return value.reshape(z * x * (y // LANES), LANES)


def from_rows(rows, shape):
    z, x, y = shape
    rows = rows.reshape(z, x // 8, y // LANES, 8, LANES).transpose(0, 1, 3, 2, 4)
    return rows.reshape(shape)


def iota(shape, axis):
    return lax.broadcasted_iota(jnp.int32, shape, axis)


def by_lanes(ref):
    return jnp.concatenate([ref[:, b, :] for b in range(ref.shape[1])], axis=1)


def ranks_of(mine):
    before_lane = (iota((LANES, LANES), 0) < iota((LANES, LANES), 1)).astype(jnp.bfloat16)
    before_row = (iota((PLANES, PLANES), 1) < iota((PLANES, PLANES), 0)).astype(jnp.bfloat16)
    all_lanes = jnp.ones((LANES, LANES), jnp.bfloat16)
    mask = jnp.where(mine, 1.0, 0.0).astype(jnp.bfloat16)
    inside = jnp.dot(mask, before_lane, preferred_element_type=jnp.float32)
    per_row = jnp.dot(mask, all_lanes, preferred_element_type=jnp.float32)
    ahead = jnp.dot(before_row, per_row.astype(jnp.bfloat16), preferred_element_type=jnp.float32)
    return jnp.where(mine, (inside + ahead).astype(jnp.int32), -1)


def compact(rank, value, empty, picked_ref):
    for block in range(CAP // 64):
        slot = iota((64, LANES), 0) + 64 * block
        picked = jnp.zeros((64, LANES), jnp.float32)
        for row in range(PLANES):
            picked = jnp.where(rank[row : row + 1, :] == slot, value[row : row + 1, :] - empty, picked)
        picked_ref[pl.ds(64 * block, 64), :] = picked
    total = lax.dot_general(
        jnp.ones((8, LANES), jnp.float32), picked_ref[...], (((1,), (1,)), ((), ())),
        precision=HIGH, preferred_element_type=jnp.float32,
    )
    return (total[0:1, :] + empty).astype(jnp.int32)


def request_kernel(
    shift_ref, tile_ref, rows_hbm, list1_ref, list2_ref, place_ref, shift_out, rows_ref, picked_ref, sem
):
    copy = pltpu.make_async_copy(rows_hbm, rows_ref, sem)
    copy.start()
    shift, tile = by_lanes(shift_ref), by_lanes(tile_ref)
    place = (tile & -64) | ((tile & 7) << 3) | (lax.shift_right_logical(tile, 3) & 7)
    place_ref[...] = place
    shift_out[...] = shift
    place = place.astype(jnp.float32)
    for step, list_ref in ((1, list1_ref), (2, list2_ref)):
        list_ref[...] = compact(ranks_of(shift == step), place, 0.0, picked_ref)
    copy.wait()


def request(shift, tile, rows):
    return pl.pallas_call(
        request_kernel,
        out_shape=(
            pltpu.VMEM((1, CAP), jnp.int32),
            pltpu.VMEM((1, CAP), jnp.int32),
            jax.ShapeDtypeStruct((PLANES, LANES), jnp.int32),
            pltpu.VMEM((PLANES, LANES), jnp.int32),
            pltpu.VMEM((TILES, LANES), jnp.float32),
        ),
        in_specs=[VMEM] * 2 + [ANY],
        out_specs=[VMEM] * 5,
        scratch_shapes=[pltpu.VMEM((CAP, LANES), jnp.float32), pltpu.SemaphoreType.DMA],
        compiler_params=PARAMS,
        name="request",
    )(far(shift), far(tile), far(rows))


def serve_kernel(list_ref, rows_ref, out_ref):
    def step(k, carry):
        for j in range(32):
            slot = k * 32 + j
            out_ref[pl.ds(slot, 1), :] = rows_ref[pl.ds(list_ref[0, slot], 1), :]
        return carry

    lax.fori_loop(0, CAP // 32, step, 0)


def serve(wanted, rows):
    return pl.pallas_call(
        serve_kernel,
        out_shape=pltpu.VMEM((CAP, LANES), jnp.float32),
        in_specs=[SMEM, VMEM],
        out_specs=VMEM,
        compiler_params=PARAMS,
        name="serve",
    )(wanted, near(rows))


def coef_kernel(diff_ref, mats_ref, own_ref, red_ref, top_ref, diag_ref, own_t, row_t):
    devices = red_ref.shape[1]
    row = lambda a, z: a[z : z + 1, :]
    lane = iota((1, LANES), 1)
    plane_of = (iota((PLANES, LANES), 1) & (PLANES - 1)) == iota((PLANES, LANES), 0)
    diff = jnp.zeros((PLANES, LANES), jnp.float32)
    per_row = LANES // PLANES
    for r in range(diff_ref.shape[0]):
        goes = iota((LANES, LANES), 1) == lax.shift_right_logical(iota((LANES, LANES), 0), 4) + per_row * r
        diff = diff + jnp.dot(
            jnp.where(plane_of, diff_ref[pl.ds(r, 1), :], 0.0), jnp.where(goes, 1.0, 0.0),
            precision=HIGH, preferred_element_type=jnp.float32,
        )
    kr = [0.5 * (row(diff, z + 1) + row(diff, z)) for z in range(PLANES - 1)]
    beyond = pltpu.roll(diff, LANES - 1, 1)
    kr.append(jnp.where(lane < devices - 1, 0.5 * (row(beyond, 0) + row(diff, PLANES - 1)), 0.0))
    kl = [jnp.where(lane > 0, pltpu.roll(jnp.broadcast_to(kr[-1], (8, LANES)), 1, 1)[0:1, :], 0.0)]
    kl = kl + kr[:-1]
    inv, low, up = [], [], []
    for z in range(PLANES):
        pivot = 1.0 + kl[z] + kr[z]
        if z > 0:
            pivot = pivot - kr[z - 1] * up[z - 1]
        inv.append(1.0 / pivot)
        low.append(jnp.zeros_like(pivot) if z == 0 else kr[z - 1] * inv[z])
        up.append(kr[z] * inv[z])
    left = [kl[0] * inv[0]]
    for z in range(1, PLANES):
        left.append(low[z] * left[z - 1])
    right = [None] * PLANES
    right[-1] = up[-1]
    for z in range(PLANES - 2, -1, -1):
        left[z] = left[z] + up[z] * left[z + 1]
        right[z] = up[z] * right[z + 1]
    mine = lane == lax.axis_index("gy")
    ones = jnp.ones((LANES, LANES), jnp.float32)
    for kind, values in enumerate((inv, low, up, left, right)):
        for z in range(PLANES):
            own_t[pl.ds(kind * PLANES + z, 1), :] = jnp.where(mine, values[z], 0.0)
    own_ref[...] = jnp.dot(own_t[...], ones, precision=HIGH, preferred_element_type=jnp.float32)
    eye = iota((devices, LANES), 0) == iota((devices, LANES), 1)
    for kind, value in enumerate((left[0], left[-1], right[0], right[-1])):
        row_t[pl.ds(kind * devices, devices), :] = jnp.where(eye, value, 0.0)
    spread = jnp.dot(row_t[...], ones, precision=HIGH, preferred_element_type=jnp.float32)
    none, all_of = jnp.zeros((1, LANES), jnp.float32), jnp.ones((1, LANES), jnp.float32)
    groups = []
    for d in range(devices):
        if d % GROUP == 0:
            ratio, to_last, to_first, l_group = none, all_of, all_of, none
        l_first, l_last, r_first, r_last = (row(spread, kind * devices + d) for kind in range(4))
        gain = 1.0 / (1.0 - l_first * ratio)
        for kind, value in enumerate(
            (
                l_last * ratio * gain, l_last * gain, gain, gain * l_first, gain * r_first, ratio,
                to_first * gain, to_first * gain * l_first,
            )
        ):
            red_ref[kind, pl.ds(d, 1), :] = value
        l_group = l_group + to_first * gain * l_first * to_last
        to_first = to_first * gain * r_first
        ratio = r_last + l_last * ratio * gain * r_first
        to_last = l_last * gain * to_last
        if d % GROUP == GROUP - 1:
            groups.append((l_group, to_last, to_first, ratio))
    ratio = none
    for g, (l_first, l_last, r_first, r_last) in enumerate(groups):
        gain = 1.0 / (1.0 - l_first * ratio)
        for kind, value in enumerate(
            (l_last * ratio * gain, l_last * gain, gain, gain * l_first, gain * r_first, ratio)
        ):
            top_ref[kind, pl.ds(g, 1), :] = value
        ratio = r_last + l_last * ratio * gain * r_first
    r, c = iota((LANES, LANES), 0), iota((LANES, LANES), 1)
    for kind, at in enumerate((r == c, r == c + 1, r == c - 1)):
        values = jnp.concatenate(
            [jnp.sum(jnp.where(at, mats_ref[m], 0.0), axis=0, keepdims=True) for m in range(NMAT)], axis=0
        )
        first = values.astype(jnp.bfloat16).astype(jnp.float32)
        second = (values - first).astype(jnp.bfloat16).astype(jnp.float32)
        third = values - first - second
        stacked = jnp.concatenate([first, second, third, jnp.zeros_like(first)], axis=0)
        diag_ref[:, pl.ds(kind * LANES, LANES)] = stacked.astype(jnp.bfloat16)


def coefficients(diffusivity, mats, devices):
    return pl.pallas_call(
        coef_kernel,
        out_shape=(
            pltpu.VMEM((5 * PLANES, LANES), jnp.float32),
            pltpu.VMEM((8, devices, LANES), jnp.float32),
            pltpu.VMEM((6, devices // GROUP, LANES), jnp.float32),
            pltpu.VMEM((4 * NMAT, 3 * LANES), jnp.bfloat16),
        ),
        in_specs=[VMEM] * 2,
        out_specs=[VMEM] * 4,
        scratch_shapes=[
            pltpu.VMEM((5 * PLANES, LANES), jnp.float32),
            pltpu.VMEM((4 * devices, LANES), jnp.float32),
        ],
        compiler_params=PARAMS,
        cost_estimate=pl.CostEstimate(flops=8_000_000, bytes_accessed=4_000_000, transcendentals=0),
        name="coefficients",
    )(diffusivity.reshape(-1, LANES), mats)


def local_kernel(
    place_ref, rows_ref, shift_ref, class_ref, diag_ref, one_hbm, two_hbm,
    dep_ref, weights_ref, to1_ref, to2_ref, one_ref, two_ref, picked_ref, sems,
):
    copies = [
        pltpu.make_async_copy(one_hbm, one_ref, sems.at[0]),
        pltpu.make_async_copy(two_hbm, two_ref, sems.at[1]),
    ]
    for copy in copies:
        copy.start()
    shift = shift_ref[...]
    spot = iota((PLANES, LANES), 1)
    spot = ((spot & 8) << 3) | (lax.shift_right_logical(spot, 4) << 3) | (spot & 7)
    spot = (spot + ROWS * iota((PLANES, LANES), 0)).astype(jnp.float32)
    for step, to_ref in ((1, to1_ref), (2, to2_ref)):
        to_ref[...] = compact(ranks_of(shift == step), spot, float(TILES), picked_ref)
    classes = by_lanes(class_ref)
    diag = diag_ref[...]
    of_class = jnp.bitwise_and(iota((4 * NMAT, ROWS), 0), NMAT - 1)
    for z in range(PLANES):
        chosen = jnp.where(of_class == classes[z : z + 1, :], 1.0, 0.0).astype(jnp.bfloat16)
        weights = lax.dot_general(
            chosen, diag, (((0,), (0,)), ((), ())), preferred_element_type=jnp.float32
        )
        for group in range(ROWS // 8):
            at = z * ROWS + (group % 2) * 64 + (group // 2) * 8
            weights_ref[pl.ds(at, 8), :] = weights[group * 8 : group * 8 + 8, :]

    def plane(z, carry):
        start = pl.multiple_of(z * ROWS, ROWS)
        for j in range(ROWS):
            at = ((j >> 3) & 1) * 64 + (j >> 4) * 8 + (j & 7)
            dep_ref[pl.ds(start + at, 1), :] = rows_ref[pl.ds(place_ref[z, j], 1), :]
        return carry

    lax.fori_loop(0, PLANES, plane, 0)
    for copy in copies:
        copy.wait()


def before_arrival(place, rows, shift, classes, diag, one, two):
    return pl.pallas_call(
        local_kernel,
        out_shape=(
            pltpu.VMEM((TILES + 8, LANES), jnp.float32),
            pltpu.VMEM((TILES, 3 * LANES), jnp.float32),
            jax.ShapeDtypeStruct((1, CAP), jnp.int32),
            jax.ShapeDtypeStruct((1, CAP), jnp.int32),
            pltpu.VMEM((TILES, LANES), jnp.float32),
            pltpu.VMEM((TILES, LANES), jnp.float32),
        ),
        in_specs=[SMEM] + [VMEM] * 4 + [ANY] * 2,
        out_specs=[VMEM] * 6,
        scratch_shapes=[pltpu.VMEM((CAP, LANES), jnp.float32), pltpu.SemaphoreType.DMA((2,))],
        compiler_params=PARAMS,
        cost_estimate=pl.CostEstimate(flops=20_000_000, bytes_accessed=10_000_000, transcendentals=0),
        name="before_arrival",
    )(place, near(rows), near(shift), classes, near(diag), far(one), far(two))


def patch_kernel(to_ref, got_ref, dep_in, dep_ref):
    del dep_in

    def patch(k, carry):
        start = pl.multiple_of(k * 32, 32)
        for j in range(32):
            dep_ref[pl.ds(to_ref[0, start + j], 1), :] = got_ref[pl.ds(start + j, 1), :]
        return carry

    lax.fori_loop(0, CAP // 32, patch, 0)


def patched(to, got, dep):
    return pl.pallas_call(
        patch_kernel,
        out_shape=pltpu.VMEM(dep.shape, jnp.float32),
        in_specs=[SMEM] + [VMEM] * 2,
        out_specs=VMEM,
        input_output_aliases={2: 0},
        compiler_params=PARAMS,
        name="patch",
    )(to, near(got), near(dep))


def slab_kernel(
    to_ref, got_ref, dep_in, weights_ref, one_ref, two_ref, own_ref, base_ref, ends_ref, dep_ref, partial
):
    patch_kernel(to_ref, got_ref, dep_in, dep_ref)

    def own(kind, z):
        return own_ref[pl.ds(kind * PLANES + z, 1), :]

    def forward(z, before):
        here = pl.ds(pl.multiple_of(z * ROWS, ROWS), ROWS)
        cells = dep_ref[here, :]
        adv = (
            weights_ref[here, pl.ds(0, LANES)] * cells
            + pltpu.roll(weights_ref[here, pl.ds(LANES, LANES)] * cells, 1, 1)
            + pltpu.roll(weights_ref[here, pl.ds(2 * LANES, LANES)] * cells, LANES - 1, 1)
        )
        a, b = 0.5 + adv, 2.0 + adv
        ab = a * b
        free = adv * ab / (ab + one_ref[here, :] * b + two_ref[here, :] * a)
        base_ref[here, :] = adv - free
        before = free * own(0, z) + before * own(1, z)
        partial[here, :] = before
        return before

    last = lax.fori_loop(0, PLANES, forward, jnp.zeros((ROWS, LANES), jnp.float32))

    def backward(k, after):
        z = PLANES - 1 - k
        here = pl.ds(pl.multiple_of(z * ROWS, ROWS), ROWS)
        after = partial[here, :] + after * own(2, z)
        base_ref[here, :] = base_ref[here, :] + after
        return after

    first = lax.fori_loop(0, PLANES, backward, jnp.zeros((ROWS, LANES), jnp.float32))
    share = ends_ref.shape[1] // 2
    for d in range(ends_ref.shape[0]):
        ends_ref[d, pl.ds(0, share), :] = first[d * share : (d + 1) * share, :]
        ends_ref[d, pl.ds(share, share), :] = last[d * share : (d + 1) * share, :]


def slab(to, got, dep, weights, one, two, own):
    base, ends, _ = pl.pallas_call(
        slab_kernel,
        out_shape=(
            pltpu.VMEM((TILES, LANES), jnp.float32),
            pltpu.VMEM((GROUP, 2 * ROWS // GROUP, LANES), jnp.float32),
            pltpu.VMEM((TILES + 8, LANES), jnp.float32),
        ),
        in_specs=[SMEM] + [VMEM] * 6,
        out_specs=[VMEM] * 3,
        scratch_shapes=[pltpu.VMEM((TILES, LANES), jnp.float32)],
        input_output_aliases={2: 2},
        compiler_params=PARAMS,
        name="slab",
    )(to, near(got), near(dep), near(weights), near(one), near(two), near(own))
    return base, ends


def inner_kernel(ends_ref, red_ref, out_ref):
    share = ends_ref.shape[1] // 2
    start = lax.axis_index("gy") // GROUP * GROUP
    coef = lambda kind, d: red_ref[kind, pl.ds(start + d, 1), :]
    top = last = jnp.zeros((share, LANES), jnp.float32)
    for d in range(GROUP):
        first = ends_ref[d, pl.ds(0, share), :]
        top = top + coef(6, d) * first + coef(7, d) * last
        last = ends_ref[d, pl.ds(share, share), :] + coef(0, d) * first + coef(1, d) * last
    for g in range(out_ref.shape[0]):
        out_ref[g, pl.ds(0, share), :] = top
        out_ref[g, pl.ds(share, share), :] = last


def inner(ends, red, groups):
    return pl.pallas_call(
        inner_kernel,
        out_shape=pltpu.VMEM((groups,) + ends.shape[1:], jnp.float32),
        in_specs=[VMEM] * 2,
        out_specs=VMEM,
        compiler_params=PARAMS,
        name="inner",
    )(near(ends), near(red))


def chain(ends_ref, coef, upto, after, carry_ref, put):
    count, both, _ = ends_ref.shape
    share = both // 2
    for d in range(count):
        first = ends_ref[d, pl.ds(0, share), :]
        carry_ref[d] = upto
        upto = ends_ref[d, pl.ds(share, share), :] + coef(0, d) * first + coef(1, d) * upto
    for d in range(count - 1, -1, -1):
        put(d, share, after)
        after = coef(2, d) * ends_ref[d, pl.ds(0, share), :] + coef(3, d) * carry_ref[d] + coef(4, d) * after
        put(d, 0, carry_ref[d] + coef(5, d) * after)


def outer_kernel(ends_ref, groups_ref, red_ref, top_ref, out_ref, sides_ref, carry_ref):
    share = ends_ref.shape[1] // 2
    group = lax.axis_index("gy") // GROUP
    zero = jnp.zeros((share, LANES), jnp.float32)

    def put_group(g, at, value):
        sides_ref[g, pl.ds(at, share), :] = value

    chain(groups_ref, lambda kind, g: top_ref[kind, pl.ds(g, 1), :], zero, zero, carry_ref, put_group)

    def put(d, at, value):
        out_ref[d, pl.ds(at, share), :] = value

    chain(
        ends_ref, lambda kind, d: red_ref[kind, pl.ds(group * GROUP + d, 1), :],
        sides_ref[group, pl.ds(0, share), :], sides_ref[group, pl.ds(share, share), :], carry_ref, put,
    )


def outer(ends, groups, red, top):
    count, both, _ = ends.shape
    return pl.pallas_call(
        outer_kernel,
        out_shape=pltpu.VMEM(ends.shape, jnp.float32),
        in_specs=[VMEM] * 4,
        out_specs=VMEM,
        scratch_shapes=[
            pltpu.VMEM(groups.shape, jnp.float32),
            pltpu.VMEM((max(count, groups.shape[0]), both // 2, LANES), jnp.float32),
        ],
        compiler_params=PARAMS,
        name="outer",
    )(near(ends), near(groups), near(red), near(top))


def exchanged(value, members):
    return lax.all_to_all(
        value, "gy", split_axis=0, concat_axis=0, tiled=True, axis_index_groups=members
    )


def finish_kernel(base_ref, near_ref, own_ref, out_ref, left_t, right_t):
    devices, both, _ = near_ref.shape
    share = both // 2
    for d in range(devices):
        left_t[pl.ds(d * share, share), :] = near_ref[d, pl.ds(0, share), :]
        right_t[pl.ds(d * share, share), :] = near_ref[d, pl.ds(share, share), :]
    left, right = left_t[...], right_t[...]
    for z in range(PLANES):
        here = pl.ds(z * ROWS, ROWS)
        from_left = own_ref[pl.ds(3 * PLANES + z, 1), :]
        from_right = own_ref[pl.ds(4 * PLANES + z, 1), :]
        out_ref[here, :] = base_ref[here, :] + from_left * left + from_right * right


def finish(base, sides, own):
    return pl.pallas_call(
        finish_kernel,
        out_shape=jax.ShapeDtypeStruct(base.shape, jnp.float32),
        in_specs=[VMEM] * 3,
        out_specs=VMEM,
        scratch_shapes=[pltpu.VMEM((ROWS, LANES), jnp.float32)] * 2,
        compiler_params=PARAMS,
        name="finish",
    )(near(base), near(sides), near(own))


def local(
    conc, target_one, target_two, diffusivity, src_shift, src_tile, interp_class, interp_mats
):
    devices = lax.axis_size("gy")
    as_stored = lambda value: value.transpose(0, 2, 1)
    list1, list2, place, shift, rows = request(as_stored(src_shift), as_stored(src_tile), to_rows(conc))
    asked2, asked1 = shifted(list2, "gx", -2), shifted(list1, "gx", -1)
    own, red, top, diag = coefficients(diffusivity, interp_mats, devices)
    got2 = shifted(serve(asked2, rows), "gx", 2)
    got1 = shifted(serve(asked1, rows), "gx", 1)
    dep, weights, to1, to2, one, two = before_arrival(
        place, rows, shift, as_stored(interp_class), diag, to_rows(target_one), to_rows(target_two)
    )
    dep = patched(to1, got1, dep)
    base, ends = slab(to2, got2, dep, weights, one, two, own)
    groups = devices // GROUP
    close = [[g * GROUP + k for k in range(GROUP)] for g in range(groups)]
    distant = [[g * GROUP + k for g in range(groups)] for k in range(GROUP)]
    ends = exchanged(ends, close)
    sides = outer(ends, exchanged(inner(ends, red, groups), distant), red, top)
    sides = exchanged(sides, close)
    return from_rows(finish(base, sides, own), conc.shape)


def solution(mesh):
    slabs = P("gy", "gx", None)
    in_specs = (slabs, slabs, slabs, P(), slabs, slabs, slabs, P())
    return jax.shard_map(local, mesh=mesh, in_specs=in_specs, out_specs=slabs, check_vma=False)
```

```python
import jax
import jax.numpy as jnp
from jax import lax
from jax.experimental import pallas as pl
from jax.experimental.pallas import tpu as pltpu
from jax.sharding import PartitionSpec as P

LANES = 128
NMAT = 8
PLANES = 16
ROWS = 128
TILES = PLANES * ROWS
CAP = 512
GROUP = 8
HIGH = lax.Precision.HIGHEST
VMEM = pl.BlockSpec(memory_space=pltpu.VMEM)
SMEM = pl.BlockSpec(memory_space=pltpu.SMEM)
ANY = pl.BlockSpec(memory_space=pl.ANY)
PARAMS = pltpu.CompilerParams(vmem_limit_bytes=24 << 20)


def near(value):
    return pltpu.with_memory_space_constraint(value, pltpu.VMEM)


def shifted(value, axis, by):
    peers = lax.axis_size(axis)
    pairs = [(i, i + by) for i in range(peers) if 0 <= i + by < peers]
    return lax.ppermute(value, axis, pairs)


def far(value):
    return pltpu.with_memory_space_constraint(value, pltpu.HBM)


def to_rows(value):
    z, x, y = value.shape
    value = value.reshape(z, x // 8, 8, y // LANES, LANES).transpose(0, 1, 3, 2, 4)
    return value.reshape(z * x * (y // LANES), LANES)


def from_rows(rows, shape):
    z, x, y = shape
    rows = rows.reshape(z, x // 8, y // LANES, 8, LANES).transpose(0, 1, 3, 2, 4)
    return rows.reshape(shape)


def iota(shape, axis):
    return lax.broadcasted_iota(jnp.int32, shape, axis)


def by_lanes(ref):
    return jnp.concatenate([ref[:, b, :] for b in range(ref.shape[1])], axis=1)


def compact(shift, value, empty, picked_ref):
    before_lane = (iota((LANES, LANES), 0) < iota((LANES, LANES), 1)).astype(jnp.bfloat16)
    before_row = (iota((PLANES, PLANES), 1) < iota((PLANES, PLANES), 0)).astype(jnp.bfloat16)
    all_lanes = jnp.ones((LANES, LANES), jnp.bfloat16)
    for step in (1, 2):
        mine = shift == step
        mask = jnp.where(mine, 1.0, 0.0).astype(jnp.bfloat16)
        inside = jnp.dot(mask, before_lane, preferred_element_type=jnp.float32)
        per_row = jnp.dot(mask, all_lanes, preferred_element_type=jnp.float32)
        ahead = jnp.dot(before_row, per_row.astype(jnp.bfloat16), preferred_element_type=jnp.float32)
        rank = jnp.where(mine, (inside + ahead).astype(jnp.int32), -1)
        for block in range(CAP // 64):
            slot = iota((64, LANES), 0) + 64 * block
            picked = jnp.zeros((64, LANES), jnp.int32)
            for row in range(PLANES):
                picked = jnp.where(
                    rank[row : row + 1, :] == slot, value[row : row + 1, :] - empty, picked
                )
            picked_ref[pl.ds((step - 1) * CAP + 64 * block, 64), :] = picked
    picked = picked_ref[...]
    low = picked & 7
    total = jnp.full((8, 2 * CAP), empty, jnp.float32)
    for part in (picked - low, low):
        total = total + lax.dot_general(
            jnp.ones((8, LANES), jnp.bfloat16), part.astype(jnp.float32).astype(jnp.bfloat16),
            (((1,), (1,)), ((), ())), preferred_element_type=jnp.float32,
        )
    return total[0:1, :].astype(jnp.int32)


def request_kernel(
    shift_ref, tile_ref, rows_hbm, list1_ref, list2_ref, place_ref, shift_out, rows_ref, picked_ref, sem
):
    copy = pltpu.make_async_copy(rows_hbm, rows_ref, sem)
    copy.start()
    shift, tile = by_lanes(shift_ref), by_lanes(tile_ref)
    place = (tile & -64) | ((tile & 7) << 3) | (lax.shift_right_logical(tile, 3) & 7)
    place_ref[...] = place
    shift_out[...] = shift
    both = compact(shift, place, 0, picked_ref)
    list1_ref[...] = both[:, :CAP]
    list2_ref[...] = both[:, CAP:]
    copy.wait()


def request(shift, tile, rows):
    return pl.pallas_call(
        request_kernel,
        out_shape=(
            pltpu.VMEM((1, CAP), jnp.int32),
            pltpu.VMEM((1, CAP), jnp.int32),
            jax.ShapeDtypeStruct((PLANES, LANES), jnp.int32),
            pltpu.VMEM((PLANES, LANES), jnp.int32),
            pltpu.VMEM((TILES, LANES), jnp.float32),
        ),
        in_specs=[VMEM] * 2 + [ANY],
        out_specs=[VMEM] * 5,
        scratch_shapes=[pltpu.VMEM((2 * CAP, LANES), jnp.int32), pltpu.SemaphoreType.DMA],
        compiler_params=PARAMS,
        name="request",
    )(far(shift), far(tile), far(rows))


def serve_kernel(list_ref, rows_ref, out_ref):
    def step(k, carry):
        for j in range(32):
            slot = k * 32 + j
            out_ref[pl.ds(slot, 1), :] = rows_ref[pl.ds(list_ref[0, slot], 1), :]
        return carry

    lax.fori_loop(0, CAP // 32, step, 0)


def serve(wanted, rows):
    return pl.pallas_call(
        serve_kernel,
        out_shape=pltpu.VMEM((CAP, LANES), jnp.float32),
        in_specs=[SMEM, VMEM],
        out_specs=VMEM,
        compiler_params=PARAMS,
        name="serve",
    )(wanted, near(rows))


def coef_kernel(diff_ref, mats_ref, own_ref, red_ref, top_ref, diag_ref, own_t, row_t):
    devices = red_ref.shape[1]
    row = lambda a, z: a[z : z + 1, :]
    lane = iota((1, LANES), 1)
    plane_of = (iota((PLANES, LANES), 1) & (PLANES - 1)) == iota((PLANES, LANES), 0)
    diff = jnp.zeros((PLANES, LANES), jnp.float32)
    per_row = LANES // PLANES
    for r in range(diff_ref.shape[0]):
        goes = iota((LANES, LANES), 1) == lax.shift_right_logical(iota((LANES, LANES), 0), 4) + per_row * r
        diff = diff + jnp.dot(
            jnp.where(plane_of, diff_ref[pl.ds(r, 1), :], 0.0), jnp.where(goes, 1.0, 0.0),
            precision=HIGH, preferred_element_type=jnp.float32,
        )
    kr = [0.5 * (row(diff, z + 1) + row(diff, z)) for z in range(PLANES - 1)]
    beyond = pltpu.roll(diff, LANES - 1, 1)
    kr.append(jnp.where(lane < devices - 1, 0.5 * (row(beyond, 0) + row(diff, PLANES - 1)), 0.0))
    kl = [jnp.where(lane > 0, pltpu.roll(jnp.broadcast_to(kr[-1], (8, LANES)), 1, 1)[0:1, :], 0.0)]
    kl = kl + kr[:-1]
    inv, low, up = [], [], []
    for z in range(PLANES):
        pivot = 1.0 + kl[z] + kr[z]
        if z > 0:
            pivot = pivot - kr[z - 1] * up[z - 1]
        inv.append(1.0 / pivot)
        low.append(jnp.zeros_like(pivot) if z == 0 else kr[z - 1] * inv[z])
        up.append(kr[z] * inv[z])
    left = [kl[0] * inv[0]]
    for z in range(1, PLANES):
        left.append(low[z] * left[z - 1])
    right = [None] * PLANES
    right[-1] = up[-1]
    for z in range(PLANES - 2, -1, -1):
        left[z] = left[z] + up[z] * left[z + 1]
        right[z] = up[z] * right[z + 1]
    mine = lane == lax.axis_index("gy")
    ones = jnp.ones((LANES, LANES), jnp.float32)
    for kind, values in enumerate((inv, low, up, left, right)):
        for z in range(PLANES):
            own_t[pl.ds(kind * PLANES + z, 1), :] = jnp.where(mine, values[z], 0.0)
    own_ref[...] = jnp.dot(own_t[...], ones, precision=HIGH, preferred_element_type=jnp.float32)
    eye = iota((devices, LANES), 0) == iota((devices, LANES), 1)
    for kind, value in enumerate((left[0], left[-1], right[0], right[-1])):
        row_t[pl.ds(kind * devices, devices), :] = jnp.where(eye, value, 0.0)
    spread = jnp.dot(row_t[...], ones, precision=HIGH, preferred_element_type=jnp.float32)
    none, all_of = jnp.zeros((1, LANES), jnp.float32), jnp.ones((1, LANES), jnp.float32)
    groups = []
    for d in range(devices):
        if d % GROUP == 0:
            ratio, to_last, to_first, l_group = none, all_of, all_of, none
        l_first, l_last, r_first, r_last = (row(spread, kind * devices + d) for kind in range(4))
        gain = 1.0 / (1.0 - l_first * ratio)
        for kind, value in enumerate(
            (
                l_last * ratio * gain, l_last * gain, gain, gain * l_first, gain * r_first, ratio,
                to_first * gain, to_first * gain * l_first,
            )
        ):
            red_ref[kind, pl.ds(d, 1), :] = value
        l_group = l_group + to_first * gain * l_first * to_last
        to_first = to_first * gain * r_first
        ratio = r_last + l_last * ratio * gain * r_first
        to_last = l_last * gain * to_last
        if d % GROUP == GROUP - 1:
            groups.append((l_group, to_last, to_first, ratio))
    ratio = none
    for g, (l_first, l_last, r_first, r_last) in enumerate(groups):
        gain = 1.0 / (1.0 - l_first * ratio)
        for kind, value in enumerate(
            (l_last * ratio * gain, l_last * gain, gain, gain * l_first, gain * r_first, ratio)
        ):
            top_ref[kind, pl.ds(g, 1), :] = value
        ratio = r_last + l_last * ratio * gain * r_first
    r, c = iota((LANES, LANES), 0), iota((LANES, LANES), 1)
    for kind, at in enumerate((r == c, r == c + 1, r == c - 1)):
        values = jnp.concatenate(
            [jnp.sum(jnp.where(at, mats_ref[m], 0.0), axis=0, keepdims=True) for m in range(NMAT)], axis=0
        )
        first = values.astype(jnp.bfloat16).astype(jnp.float32)
        second = (values - first).astype(jnp.bfloat16).astype(jnp.float32)
        third = values - first - second
        stacked = jnp.concatenate([first, second, third, jnp.zeros_like(first)], axis=0)
        diag_ref[:, pl.ds(kind * LANES, LANES)] = stacked.astype(jnp.bfloat16)


def coefficients(diffusivity, mats, devices):
    return pl.pallas_call(
        coef_kernel,
        out_shape=(
            pltpu.VMEM((5 * PLANES, LANES), jnp.float32),
            pltpu.VMEM((8, devices, LANES), jnp.float32),
            pltpu.VMEM((6, devices // GROUP, LANES), jnp.float32),
            pltpu.VMEM((4 * NMAT, 3 * LANES), jnp.bfloat16),
        ),
        in_specs=[VMEM] * 2,
        out_specs=[VMEM] * 4,
        scratch_shapes=[
            pltpu.VMEM((5 * PLANES, LANES), jnp.float32),
            pltpu.VMEM((4 * devices, LANES), jnp.float32),
        ],
        compiler_params=PARAMS,
        cost_estimate=pl.CostEstimate(flops=8_000_000, bytes_accessed=4_000_000, transcendentals=0),
        name="coefficients",
    )(diffusivity.reshape(-1, LANES), mats)


def local_kernel(
    place_ref, rows_ref, shift_ref, class_ref, diag_ref, one_hbm, two_hbm,
    dep_ref, weights_ref, to1_ref, to2_ref, one_ref, two_ref, picked_ref, sems,
):
    copies = [
        pltpu.make_async_copy(one_hbm, one_ref, sems.at[0]),
        pltpu.make_async_copy(two_hbm, two_ref, sems.at[1]),
    ]
    for copy in copies:
        copy.start()
    shift = shift_ref[...]
    spot = iota((PLANES, LANES), 1)
    spot = ((spot & 8) << 3) | (lax.shift_right_logical(spot, 4) << 3) | (spot & 7)
    both = compact(shift, spot + ROWS * iota((PLANES, LANES), 0), TILES, picked_ref)
    to1_ref[...] = both[:, :CAP]
    to2_ref[...] = both[:, CAP:]
    classes = by_lanes(class_ref)
    diag = diag_ref[...]
    of_class = jnp.bitwise_and(iota((4 * NMAT, ROWS), 0), NMAT - 1)
    for z in range(PLANES):
        chosen = jnp.where(of_class == classes[z : z + 1, :], 1.0, 0.0).astype(jnp.bfloat16)
        weights = lax.dot_general(
            chosen, diag, (((0,), (0,)), ((), ())), preferred_element_type=jnp.float32
        )
        for group in range(ROWS // 8):
            at = z * ROWS + (group % 2) * 64 + (group // 2) * 8
            weights_ref[pl.ds(at, 8), :] = weights[group * 8 : group * 8 + 8, :]

    def plane(z, carry):
        start = pl.multiple_of(z * ROWS, ROWS)
        for j in range(ROWS):
            at = ((j >> 3) & 1) * 64 + (j >> 4) * 8 + (j & 7)
            dep_ref[pl.ds(start + at, 1), :] = rows_ref[pl.ds(place_ref[z, j], 1), :]
        return carry

    lax.fori_loop(0, PLANES, plane, 0)
    for copy in copies:
        copy.wait()


def before_arrival(place, rows, shift, classes, diag, one, two):
    return pl.pallas_call(
        local_kernel,
        out_shape=(
            pltpu.VMEM((TILES + 8, LANES), jnp.float32),
            pltpu.VMEM((TILES, 3 * LANES), jnp.float32),
            jax.ShapeDtypeStruct((1, CAP), jnp.int32),
            jax.ShapeDtypeStruct((1, CAP), jnp.int32),
            pltpu.VMEM((TILES, LANES), jnp.float32),
            pltpu.VMEM((TILES, LANES), jnp.float32),
        ),
        in_specs=[SMEM] + [VMEM] * 4 + [ANY] * 2,
        out_specs=[VMEM] * 6,
        scratch_shapes=[pltpu.VMEM((2 * CAP, LANES), jnp.int32), pltpu.SemaphoreType.DMA((2,))],
        compiler_params=PARAMS,
        cost_estimate=pl.CostEstimate(flops=20_000_000, bytes_accessed=10_000_000, transcendentals=0),
        name="before_arrival",
    )(place, near(rows), near(shift), classes, near(diag), far(one), far(two))


def turned():
    half = lax.axis_size("gy") // (2 * GROUP)
    return jnp.where(lax.axis_index("gy") // GROUP >= half, GROUP // 2, 0)


def patch_kernel(to_ref, got_ref, dep_in, dep_ref):
    del dep_in

    def patch(k, carry):
        start = pl.multiple_of(k * 32, 32)
        for j in range(32):
            dep_ref[pl.ds(to_ref[0, start + j], 1), :] = got_ref[pl.ds(start + j, 1), :]
        return carry

    lax.fori_loop(0, CAP // 32, patch, 0)


def patched(to, got, dep):
    return pl.pallas_call(
        patch_kernel,
        out_shape=pltpu.VMEM(dep.shape, jnp.float32),
        in_specs=[SMEM] + [VMEM] * 2,
        out_specs=VMEM,
        input_output_aliases={2: 0},
        compiler_params=PARAMS,
        name="patch",
    )(to, near(got), near(dep))


def slab_kernel(
    to_ref, got_ref, dep_in, weights_ref, one_ref, two_ref, own_ref, base_ref, ends_ref, dep_ref, partial
):
    patch_kernel(to_ref, got_ref, dep_in, dep_ref)

    def own(kind, z):
        return own_ref[pl.ds(kind * PLANES + z, 1), :]

    def forward(z, before):
        here = pl.ds(z * ROWS, ROWS)
        cells = dep_ref[here, :]
        adv = (
            weights_ref[here, pl.ds(0, LANES)] * cells
            + pltpu.roll(weights_ref[here, pl.ds(LANES, LANES)] * cells, 1, 1)
            + pltpu.roll(weights_ref[here, pl.ds(2 * LANES, LANES)] * cells, LANES - 1, 1)
        )
        a, b = 0.5 + adv, 2.0 + adv
        ab = a * b
        free = adv * ab / (ab + one_ref[here, :] * b + two_ref[here, :] * a)
        base_ref[here, :] = adv - free
        before = free * own(0, z) + before * own(1, z)
        partial[here, :] = before
        return before

    last = jnp.zeros((ROWS, LANES), jnp.float32)
    for z in range(PLANES):
        last = forward(z, last)

    def backward(k, after):
        z = PLANES - 1 - k
        here = pl.ds(z * ROWS, ROWS)
        after = partial[here, :] + after * own(2, z)
        base_ref[here, :] = base_ref[here, :] + after
        return after

    first = jnp.zeros((ROWS, LANES), jnp.float32)
    for k in range(PLANES):
        first = backward(k, first)
    share = ends_ref.shape[1] // 2
    turn = turned()
    for d in range(ends_ref.shape[0]):
        ends_ref[d ^ turn, pl.ds(0, share), :] = first[d * share : (d + 1) * share, :]
        ends_ref[d ^ turn, pl.ds(share, share), :] = last[d * share : (d + 1) * share, :]


def slab(to, got, dep, weights, one, two, own):
    base, ends, _ = pl.pallas_call(
        slab_kernel,
        out_shape=(
            pltpu.VMEM((TILES, LANES), jnp.float32),
            pltpu.VMEM((GROUP, 2 * ROWS // GROUP, LANES), jnp.float32),
            pltpu.VMEM((TILES + 8, LANES), jnp.float32),
        ),
        in_specs=[SMEM] + [VMEM] * 6,
        out_specs=[VMEM] * 3,
        scratch_shapes=[pltpu.VMEM((TILES, LANES), jnp.float32)],
        input_output_aliases={2: 2},
        compiler_params=PARAMS,
        name="slab",
    )(to, near(got), near(dep), near(weights), near(one), near(two), near(own))
    return base, ends


def inner_kernel(ends_ref, red_ref, out_ref):
    share = ends_ref.shape[1] // 2
    start = lax.axis_index("gy") // GROUP * GROUP
    coef = lambda kind, d: red_ref[kind, pl.ds(start + d, 1), :]
    top = last = jnp.zeros((share, LANES), jnp.float32)
    for d in range(GROUP):
        first = ends_ref[d, pl.ds(0, share), :]
        top = top + coef(6, d) * first + coef(7, d) * last
        last = ends_ref[d, pl.ds(share, share), :] + coef(0, d) * first + coef(1, d) * last
    for g in range(out_ref.shape[0]):
        out_ref[g, pl.ds(0, share), :] = top
        out_ref[g, pl.ds(share, share), :] = last


def inner(ends, red, groups):
    return pl.pallas_call(
        inner_kernel,
        out_shape=pltpu.VMEM((groups,) + ends.shape[1:], jnp.float32),
        in_specs=[VMEM] * 2,
        out_specs=VMEM,
        compiler_params=PARAMS,
        name="inner",
    )(near(ends), near(red))


def chain(ends_ref, coef, upto, after, carry_ref, put):
    count, both, _ = ends_ref.shape
    share = both // 2
    for d in range(count):
        first = ends_ref[d, pl.ds(0, share), :]
        carry_ref[d] = upto
        upto = ends_ref[d, pl.ds(share, share), :] + coef(0, d) * first + coef(1, d) * upto
    for d in range(count - 1, -1, -1):
        put(d, share, after)
        after = coef(2, d) * ends_ref[d, pl.ds(0, share), :] + coef(3, d) * carry_ref[d] + coef(4, d) * after
        put(d, 0, carry_ref[d] + coef(5, d) * after)


def outer_kernel(ends_ref, groups_ref, red_ref, top_ref, out_ref, sides_ref, carry_ref):
    share = ends_ref.shape[1] // 2
    group = lax.axis_index("gy") // GROUP
    zero = jnp.zeros((share, LANES), jnp.float32)

    def put_group(g, at, value):
        sides_ref[g, pl.ds(at, share), :] = value

    chain(groups_ref, lambda kind, g: top_ref[kind, pl.ds(g, 1), :], zero, zero, carry_ref, put_group)

    def put(d, at, value):
        out_ref[d, pl.ds(at, share), :] = value

    chain(
        ends_ref, lambda kind, d: red_ref[kind, pl.ds(group * GROUP + d, 1), :],
        sides_ref[group, pl.ds(0, share), :], sides_ref[group, pl.ds(share, share), :], carry_ref, put,
    )


def outer(ends, groups, red, top):
    count, both, _ = ends.shape
    return pl.pallas_call(
        outer_kernel,
        out_shape=pltpu.VMEM(ends.shape, jnp.float32),
        in_specs=[VMEM] * 4,
        out_specs=VMEM,
        scratch_shapes=[
            pltpu.VMEM(groups.shape, jnp.float32),
            pltpu.VMEM((max(count, groups.shape[0]), both // 2, LANES), jnp.float32),
        ],
        compiler_params=PARAMS,
        name="outer",
    )(near(ends), near(groups), near(red), near(top))


def exchanged(value, members):
    return lax.all_to_all(
        value, "gy", split_axis=0, concat_axis=0, tiled=True, axis_index_groups=members
    )


def finish_kernel(base_ref, near_ref, own_ref, out_hbm, left_t, right_t, out_t, sems):
    devices, both, _ = near_ref.shape
    share = both // 2
    turn = turned()
    for d in range(devices):
        left_t[pl.ds(d * share, share), :] = near_ref[d ^ turn, pl.ds(0, share), :]
        right_t[pl.ds(d * share, share), :] = near_ref[d ^ turn, pl.ds(share, share), :]
    left, right = left_t[...], right_t[...]
    copies = []
    for z in range(PLANES):
        here = pl.ds(z * ROWS, ROWS)
        from_left = own_ref[pl.ds(3 * PLANES + z, 1), :]
        from_right = own_ref[pl.ds(4 * PLANES + z, 1), :]
        out_t[here, :] = base_ref[here, :] + from_left * left + from_right * right
        if z % 4 == 3:
            part = pl.ds((z - 3) * ROWS, 4 * ROWS)
            copies.append(pltpu.make_async_copy(out_t.at[part], out_hbm.at[part], sems.at[z // 4]))
            copies[-1].start()
    for copy in copies:
        copy.wait()


def finish(base, sides, own):
    return pl.pallas_call(
        finish_kernel,
        out_shape=jax.ShapeDtypeStruct(base.shape, jnp.float32),
        in_specs=[VMEM] * 3,
        out_specs=ANY,
        scratch_shapes=[pltpu.VMEM((ROWS, LANES), jnp.float32)] * 2
        + [pltpu.VMEM((TILES, LANES), jnp.float32), pltpu.SemaphoreType.DMA((PLANES // 4,))],
        compiler_params=PARAMS,
        name="finish",
    )(near(base), near(sides), near(own))


def local(
    conc, target_one, target_two, diffusivity, src_shift, src_tile, interp_class, interp_mats
):
    devices = lax.axis_size("gy")
    as_stored = lambda value: value.transpose(0, 2, 1)
    list1, list2, place, shift, rows = request(as_stored(src_shift), as_stored(src_tile), to_rows(conc))
    asked2, asked1 = shifted(list2, "gx", -2), shifted(list1, "gx", -1)
    own, red, top, diag = coefficients(diffusivity, interp_mats, devices)
    got2 = shifted(serve(asked2, rows), "gx", 2)
    got1 = shifted(serve(asked1, rows), "gx", 1)
    dep, weights, to1, to2, one, two = before_arrival(
        place, rows, shift, as_stored(interp_class), diag, to_rows(target_one), to_rows(target_two)
    )
    dep = patched(to1, got1, dep)
    base, ends = slab(to2, got2, dep, weights, one, two, own)
    groups = devices // GROUP
    close = [[g * GROUP + k for k in range(GROUP)] for g in range(groups)]
    turn = [0 if g < groups // 2 else GROUP // 2 for g in range(groups)]
    distant = [[g * GROUP + (k ^ turn[g]) for g in range(groups)] for k in range(GROUP)]
    ends = exchanged(ends, close)
    sides = outer(ends, exchanged(inner(ends, red, groups), distant), red, top)
    sides = exchanged(sides, close)
    return from_rows(finish(base, sides, own), conc.shape)


def solution(mesh):
    slabs = P("gy", "gx", None)
    in_specs = (slabs, slabs, slabs, P(), slabs, slabs, slabs, P())
    return jax.shard_map(local, mesh=mesh, in_specs=in_specs, out_specs=slabs, check_vma=False)
```

```python
import jax
import jax.numpy as jnp
from jax import lax
from jax.experimental import pallas as pl
from jax.experimental.pallas import tpu as pltpu
from jax.sharding import PartitionSpec as P

LANES = 128
NMAT = 8
PLANES = 16
ROWS = 128
TILES = PLANES * ROWS
CAP = 512
GROUP = 8
HIGH = lax.Precision.HIGHEST
VMEM = pl.BlockSpec(memory_space=pltpu.VMEM)
SMEM = pl.BlockSpec(memory_space=pltpu.SMEM)
ANY = pl.BlockSpec(memory_space=pl.ANY)
PARAMS = pltpu.CompilerParams(vmem_limit_bytes=24 << 20)


def near(value):
    return pltpu.with_memory_space_constraint(value, pltpu.VMEM)


def shifted(value, axis, by):
    peers = lax.axis_size(axis)
    pairs = [(i, i + by) for i in range(peers) if 0 <= i + by < peers]
    return lax.ppermute(value, axis, pairs)


def far(value):
    return pltpu.with_memory_space_constraint(value, pltpu.HBM)


def to_rows(value):
    z, x, y = value.shape
    value = value.reshape(z, x // 8, 8, y // LANES, LANES).transpose(0, 1, 3, 2, 4)
    return value.reshape(z * x * (y // LANES), LANES)


def from_rows(rows, shape):
    z, x, y = shape
    rows = rows.reshape(z, x // 8, y // LANES, 8, LANES).transpose(0, 1, 3, 2, 4)
    return rows.reshape(shape)


def iota(shape, axis):
    return lax.broadcasted_iota(jnp.int32, shape, axis)


def by_lanes(ref):
    return jnp.concatenate([ref[:, b, :] for b in range(ref.shape[1])], axis=1)


def compact(shift, value, empty, picked_ref):
    before_lane = (iota((LANES, LANES), 0) < iota((LANES, LANES), 1)).astype(jnp.bfloat16)
    before_row = (iota((PLANES, PLANES), 1) < iota((PLANES, PLANES), 0)).astype(jnp.bfloat16)
    all_lanes = jnp.ones((LANES, LANES), jnp.bfloat16)
    for step in (1, 2):
        mine = shift == step
        mask = jnp.where(mine, 1.0, 0.0).astype(jnp.bfloat16)
        inside = jnp.dot(mask, before_lane, preferred_element_type=jnp.float32)
        per_row = jnp.dot(mask, all_lanes, preferred_element_type=jnp.float32)
        ahead = jnp.dot(before_row, per_row.astype(jnp.bfloat16), preferred_element_type=jnp.float32)
        rank = jnp.where(mine, (inside + ahead).astype(jnp.int32), -1)
        for block in range(CAP // 64):
            slot = iota((64, LANES), 0) + 64 * block
            picked = jnp.zeros((64, LANES), jnp.int32)
            for row in range(PLANES):
                picked = jnp.where(
                    rank[row : row + 1, :] == slot, value[row : row + 1, :] - empty, picked
                )
            picked_ref[pl.ds((step - 1) * CAP + 64 * block, 64), :] = picked
    picked = picked_ref[...]
    low = picked & 7
    total = jnp.full((8, 2 * CAP), empty, jnp.float32)
    for part in (picked - low, low):
        total = total + lax.dot_general(
            jnp.ones((8, LANES), jnp.bfloat16), part.astype(jnp.float32).astype(jnp.bfloat16),
            (((1,), (1,)), ((), ())), preferred_element_type=jnp.float32,
        )
    return total[0:1, :].astype(jnp.int32)


def request_kernel(
    shift_ref, tile_ref, rows_hbm, list1_ref, list2_ref, place_ref, shift_out, rows_ref, picked_ref, sem
):
    copy = pltpu.make_async_copy(rows_hbm, rows_ref, sem)
    copy.start()
    shift, tile = by_lanes(shift_ref), by_lanes(tile_ref)
    place = (tile & -64) | ((tile & 7) << 3) | (lax.shift_right_logical(tile, 3) & 7)
    place_ref[...] = place
    shift_out[...] = shift
    both = compact(shift, place, 0, picked_ref)
    list1_ref[...] = both[:, :CAP]
    list2_ref[...] = both[:, CAP:]
    copy.wait()


def request(shift, tile, rows):
    return pl.pallas_call(
        request_kernel,
        out_shape=(
            pltpu.VMEM((1, CAP), jnp.int32),
            pltpu.VMEM((1, CAP), jnp.int32),
            jax.ShapeDtypeStruct((PLANES, LANES), jnp.int32),
            pltpu.VMEM((PLANES, LANES), jnp.int32),
            pltpu.VMEM((TILES, LANES), jnp.float32),
        ),
        in_specs=[VMEM] * 2 + [ANY],
        out_specs=[VMEM] * 5,
        scratch_shapes=[pltpu.VMEM((2 * CAP, LANES), jnp.int32), pltpu.SemaphoreType.DMA],
        compiler_params=PARAMS,
        name="request",
    )(far(shift), far(tile), far(rows))


def serve_kernel(list_ref, rows_ref, out_ref):
    def step(k, carry):
        for j in range(32):
            slot = k * 32 + j
            out_ref[pl.ds(slot, 1), :] = rows_ref[pl.ds(list_ref[0, slot], 1), :]
        return carry

    lax.fori_loop(0, CAP // 32, step, 0)


def serve(wanted, rows):
    return pl.pallas_call(
        serve_kernel,
        out_shape=pltpu.VMEM((CAP, LANES), jnp.float32),
        in_specs=[SMEM, VMEM],
        out_specs=VMEM,
        compiler_params=PARAMS,
        name="serve",
    )(wanted, near(rows))


def coef_kernel(diff_ref, mats_ref, own_ref, red_ref, top_ref, diag_ref, own_t, row_t):
    devices = red_ref.shape[1]
    row = lambda a, z: a[z : z + 1, :]
    lane = iota((1, LANES), 1)
    plane_of = (iota((PLANES, LANES), 1) & (PLANES - 1)) == iota((PLANES, LANES), 0)
    diff = jnp.zeros((PLANES, LANES), jnp.float32)
    per_row = LANES // PLANES
    for r in range(diff_ref.shape[0]):
        goes = iota((LANES, LANES), 1) == lax.shift_right_logical(iota((LANES, LANES), 0), 4) + per_row * r
        diff = diff + jnp.dot(
            jnp.where(plane_of, diff_ref[pl.ds(r, 1), :], 0.0), jnp.where(goes, 1.0, 0.0),
            precision=HIGH, preferred_element_type=jnp.float32,
        )
    kr = [0.5 * (row(diff, z + 1) + row(diff, z)) for z in range(PLANES - 1)]
    beyond = pltpu.roll(diff, LANES - 1, 1)
    kr.append(jnp.where(lane < devices - 1, 0.5 * (row(beyond, 0) + row(diff, PLANES - 1)), 0.0))
    kl = [jnp.where(lane > 0, pltpu.roll(jnp.broadcast_to(kr[-1], (8, LANES)), 1, 1)[0:1, :], 0.0)]
    kl = kl + kr[:-1]
    inv, low, up = [], [], []
    for z in range(PLANES):
        pivot = 1.0 + kl[z] + kr[z]
        if z > 0:
            pivot = pivot - kr[z - 1] * up[z - 1]
        inv.append(1.0 / pivot)
        low.append(jnp.zeros_like(pivot) if z == 0 else kr[z - 1] * inv[z])
        up.append(kr[z] * inv[z])
    left = [kl[0] * inv[0]]
    for z in range(1, PLANES):
        left.append(low[z] * left[z - 1])
    right = [None] * PLANES
    right[-1] = up[-1]
    for z in range(PLANES - 2, -1, -1):
        left[z] = left[z] + up[z] * left[z + 1]
        right[z] = up[z] * right[z + 1]
    mine = lane == lax.axis_index("gy")
    ones = jnp.ones((LANES, LANES), jnp.float32)
    for kind, values in enumerate((inv, low, up, left, right)):
        for z in range(PLANES):
            own_t[pl.ds(kind * PLANES + z, 1), :] = jnp.where(mine, values[z], 0.0)
    own_ref[...] = jnp.dot(own_t[...], ones, precision=HIGH, preferred_element_type=jnp.float32)
    eye = iota((devices, LANES), 0) == iota((devices, LANES), 1)
    for kind, value in enumerate((left[0], left[-1], right[0], right[-1])):
        row_t[pl.ds(kind * devices, devices), :] = jnp.where(eye, value, 0.0)
    spread = jnp.dot(row_t[...], ones, precision=HIGH, preferred_element_type=jnp.float32)
    none, all_of = jnp.zeros((1, LANES), jnp.float32), jnp.ones((1, LANES), jnp.float32)
    groups = []
    for d in range(devices):
        if d % GROUP == 0:
            ratio, to_last, to_first, l_group = none, all_of, all_of, none
        l_first, l_last, r_first, r_last = (row(spread, kind * devices + d) for kind in range(4))
        gain = 1.0 / (1.0 - l_first * ratio)
        for kind, value in enumerate(
            (
                l_last * ratio * gain, l_last * gain, gain, gain * l_first, gain * r_first, ratio,
                to_first * gain, to_first * gain * l_first,
            )
        ):
            red_ref[kind, pl.ds(d, 1), :] = value
        l_group = l_group + to_first * gain * l_first * to_last
        to_first = to_first * gain * r_first
        ratio = r_last + l_last * ratio * gain * r_first
        to_last = l_last * gain * to_last
        if d % GROUP == GROUP - 1:
            groups.append((l_group, to_last, to_first, ratio))
    ratio = none
    for g, (l_first, l_last, r_first, r_last) in enumerate(groups):
        gain = 1.0 / (1.0 - l_first * ratio)
        for kind, value in enumerate(
            (l_last * ratio * gain, l_last * gain, gain, gain * l_first, gain * r_first, ratio)
        ):
            top_ref[kind, pl.ds(g, 1), :] = value
        ratio = r_last + l_last * ratio * gain * r_first
    r, c = iota((LANES, LANES), 0), iota((LANES, LANES), 1)
    for kind, at in enumerate((r == c, r == c + 1, r == c - 1)):
        values = jnp.concatenate(
            [jnp.sum(jnp.where(at, mats_ref[m], 0.0), axis=0, keepdims=True) for m in range(NMAT)], axis=0
        )
        first = values.astype(jnp.bfloat16).astype(jnp.float32)
        second = (values - first).astype(jnp.bfloat16).astype(jnp.float32)
        third = values - first - second
        stacked = jnp.concatenate([first, second, third, jnp.zeros_like(first)], axis=0)
        diag_ref[:, pl.ds(kind * LANES, LANES)] = stacked.astype(jnp.bfloat16)


def coefficients(diffusivity, mats, devices):
    return pl.pallas_call(
        coef_kernel,
        out_shape=(
            pltpu.VMEM((5 * PLANES, LANES), jnp.float32),
            pltpu.VMEM((8, devices, LANES), jnp.float32),
            pltpu.VMEM((6, devices // GROUP, LANES), jnp.float32),
            pltpu.VMEM((4 * NMAT, 3 * LANES), jnp.bfloat16),
        ),
        in_specs=[VMEM] * 2,
        out_specs=[VMEM] * 4,
        scratch_shapes=[
            pltpu.VMEM((5 * PLANES, LANES), jnp.float32),
            pltpu.VMEM((4 * devices, LANES), jnp.float32),
        ],
        compiler_params=PARAMS,
        cost_estimate=pl.CostEstimate(flops=8_000_000, bytes_accessed=4_000_000, transcendentals=0),
        name="coefficients",
    )(diffusivity.reshape(-1, LANES), mats)


def local_kernel(
    place_ref, rows_ref, shift_ref, class_ref, diag_ref, one_hbm, two_hbm,
    dep_ref, weights_ref, to1_ref, to2_ref, one_ref, two_ref, picked_ref, to_t, sems,
):
    copies = [
        pltpu.make_async_copy(one_hbm, one_ref, sems.at[0]),
        pltpu.make_async_copy(two_hbm, two_ref, sems.at[1]),
    ]
    for copy in copies:
        copy.start()
    shift = shift_ref[...]
    spot = iota((PLANES, LANES), 1)
    spot = ((spot & 8) << 3) | (lax.shift_right_logical(spot, 4) << 3) | (spot & 7)
    both = compact(shift, spot + ROWS * iota((PLANES, LANES), 0), TILES, picked_ref)
    to_t[...] = both
    copies = copies + [
        pltpu.make_async_copy(to_t.at[:, pl.ds(0, CAP)], to1_ref, sems.at[2]),
        pltpu.make_async_copy(to_t.at[:, pl.ds(CAP, CAP)], to2_ref, sems.at[3]),
    ]
    for copy in copies[2:]:
        copy.start()
    classes = by_lanes(class_ref)
    diag = diag_ref[...]
    of_class = jnp.bitwise_and(iota((4 * NMAT, ROWS), 0), NMAT - 1)
    for z in range(PLANES):
        chosen = jnp.where(of_class == classes[z : z + 1, :], 1.0, 0.0).astype(jnp.bfloat16)
        weights = lax.dot_general(
            chosen, diag, (((0,), (0,)), ((), ())), preferred_element_type=jnp.float32
        )
        for group in range(ROWS // 8):
            at = z * ROWS + (group % 2) * 64 + (group // 2) * 8
            weights_ref[pl.ds(at, 8), :] = weights[group * 8 : group * 8 + 8, :]

    def plane(z, carry):
        start = pl.multiple_of(z * ROWS, ROWS)
        for j in range(ROWS):
            at = ((j >> 3) & 1) * 64 + (j >> 4) * 8 + (j & 7)
            dep_ref[pl.ds(start + at, 1), :] = rows_ref[pl.ds(place_ref[z, j], 1), :]
        return carry

    lax.fori_loop(0, PLANES, plane, 0)
    for copy in copies:
        copy.wait()


def before_arrival(place, rows, shift, classes, diag, one, two):
    return pl.pallas_call(
        local_kernel,
        out_shape=(
            pltpu.VMEM((TILES + 8, LANES), jnp.float32),
            pltpu.VMEM((TILES, 3 * LANES), jnp.float32),
            pltpu.SMEM((1, CAP), jnp.int32),
            pltpu.SMEM((1, CAP), jnp.int32),
            pltpu.VMEM((TILES, LANES), jnp.float32),
            pltpu.VMEM((TILES, LANES), jnp.float32),
        ),
        in_specs=[SMEM] + [VMEM] * 4 + [ANY] * 2,
        out_specs=[VMEM] * 2 + [SMEM] * 2 + [VMEM] * 2,
        scratch_shapes=[
            pltpu.VMEM((2 * CAP, LANES), jnp.int32),
            pltpu.VMEM((1, 2 * CAP), jnp.int32),
            pltpu.SemaphoreType.DMA((4,)),
        ],
        compiler_params=PARAMS,
        cost_estimate=pl.CostEstimate(flops=20_000_000, bytes_accessed=10_000_000, transcendentals=0),
        name="before_arrival",
    )(place, near(rows), near(shift), classes, near(diag), far(one), far(two))


def turned():
    half = lax.axis_size("gy") // (2 * GROUP)
    return jnp.where(lax.axis_index("gy") // GROUP >= half, GROUP // 2, 0)


def patch_kernel(to_ref, got_ref, dep_in, dep_ref):
    del dep_in

    def patch(k, carry):
        start = pl.multiple_of(k * 32, 32)
        for j in range(32):
            dep_ref[pl.ds(to_ref[0, start + j], 1), :] = got_ref[pl.ds(start + j, 1), :]
        return carry

    lax.fori_loop(0, CAP // 32, patch, 0)


def patched(to, got, dep):
    return pl.pallas_call(
        patch_kernel,
        out_shape=pltpu.VMEM(dep.shape, jnp.float32),
        in_specs=[SMEM] + [VMEM] * 2,
        out_specs=VMEM,
        input_output_aliases={2: 0},
        compiler_params=PARAMS,
        name="patch",
    )(pltpu.with_memory_space_constraint(to, pltpu.SMEM), near(got), near(dep))


def slab_kernel(
    to_ref, got_ref, dep_in, weights_ref, one_ref, two_ref, own_ref, base_ref, ends_ref, dep_ref, partial
):
    patch_kernel(to_ref, got_ref, dep_in, dep_ref)

    def own(kind, z):
        return own_ref[pl.ds(kind * PLANES + z, 1), :]

    def forward(z, before):
        here = pl.ds(z * ROWS, ROWS)
        cells = dep_ref[here, :]
        adv = (
            weights_ref[here, pl.ds(0, LANES)] * cells
            + pltpu.roll(weights_ref[here, pl.ds(LANES, LANES)] * cells, 1, 1)
            + pltpu.roll(weights_ref[here, pl.ds(2 * LANES, LANES)] * cells, LANES - 1, 1)
        )
        a, b = 0.5 + adv, 2.0 + adv
        ab = a * b
        free = adv * ab / (ab + one_ref[here, :] * b + two_ref[here, :] * a)
        base_ref[here, :] = adv - free
        before = free * own(0, z) + before * own(1, z)
        partial[here, :] = before
        return before

    last = jnp.zeros((ROWS, LANES), jnp.float32)
    for z in range(PLANES):
        last = forward(z, last)

    def backward(k, after):
        z = PLANES - 1 - k
        here = pl.ds(z * ROWS, ROWS)
        after = partial[here, :] + after * own(2, z)
        base_ref[here, :] = base_ref[here, :] + after
        return after

    first = jnp.zeros((ROWS, LANES), jnp.float32)
    for k in range(PLANES):
        first = backward(k, first)
    share = ends_ref.shape[1] // 2
    turn = turned()
    for d in range(ends_ref.shape[0]):
        ends_ref[d ^ turn, pl.ds(0, share), :] = first[d * share : (d + 1) * share, :]
        ends_ref[d ^ turn, pl.ds(share, share), :] = last[d * share : (d + 1) * share, :]


def slab(to, got, dep, weights, one, two, own):
    base, ends, _ = pl.pallas_call(
        slab_kernel,
        out_shape=(
            pltpu.VMEM((TILES, LANES), jnp.float32),
            pltpu.VMEM((GROUP, 2 * ROWS // GROUP, LANES), jnp.float32),
            pltpu.VMEM((TILES + 8, LANES), jnp.float32),
        ),
        in_specs=[SMEM] + [VMEM] * 6,
        out_specs=[VMEM] * 3,
        scratch_shapes=[pltpu.VMEM((TILES, LANES), jnp.float32)],
        input_output_aliases={2: 2},
        compiler_params=PARAMS,
        name="slab",
    )(
        pltpu.with_memory_space_constraint(to, pltpu.SMEM), near(got), near(dep), near(weights), near(one), near(two), near(own))
    return base, ends


def inner_kernel(ends_ref, red_ref, out_ref):
    share = ends_ref.shape[1] // 2
    start = lax.axis_index("gy") // GROUP * GROUP
    coef = lambda kind, d: red_ref[kind, pl.ds(start + d, 1), :]
    top = last = jnp.zeros((share, LANES), jnp.float32)
    for d in range(GROUP):
        first = ends_ref[d, pl.ds(0, share), :]
        top = top + coef(6, d) * first + coef(7, d) * last
        last = ends_ref[d, pl.ds(share, share), :] + coef(0, d) * first + coef(1, d) * last
    for g in range(out_ref.shape[0]):
        out_ref[g, pl.ds(0, share), :] = top
        out_ref[g, pl.ds(share, share), :] = last


def inner(ends, red, groups):
    return pl.pallas_call(
        inner_kernel,
        out_shape=pltpu.VMEM((groups,) + ends.shape[1:], jnp.float32),
        in_specs=[VMEM] * 2,
        out_specs=VMEM,
        compiler_params=PARAMS,
        name="inner",
    )(near(ends), near(red))


def chain(ends_ref, coef, upto, after, carry_ref, put):
    count, both, _ = ends_ref.shape
    share = both // 2
    for d in range(count):
        first = ends_ref[d, pl.ds(0, share), :]
        carry_ref[d] = upto
        upto = ends_ref[d, pl.ds(share, share), :] + coef(0, d) * first + coef(1, d) * upto
    for d in range(count - 1, -1, -1):
        put(d, share, after)
        after = coef(2, d) * ends_ref[d, pl.ds(0, share), :] + coef(3, d) * carry_ref[d] + coef(4, d) * after
        put(d, 0, carry_ref[d] + coef(5, d) * after)


def outer_kernel(ends_ref, groups_ref, red_ref, top_ref, out_ref, sides_ref, carry_ref):
    share = ends_ref.shape[1] // 2
    group = lax.axis_index("gy") // GROUP
    zero = jnp.zeros((share, LANES), jnp.float32)

    def put_group(g, at, value):
        sides_ref[g, pl.ds(at, share), :] = value

    chain(groups_ref, lambda kind, g: top_ref[kind, pl.ds(g, 1), :], zero, zero, carry_ref, put_group)

    def put(d, at, value):
        out_ref[d, pl.ds(at, share), :] = value

    chain(
        ends_ref, lambda kind, d: red_ref[kind, pl.ds(group * GROUP + d, 1), :],
        sides_ref[group, pl.ds(0, share), :], sides_ref[group, pl.ds(share, share), :], carry_ref, put,
    )


def outer(ends, groups, red, top):
    count, both, _ = ends.shape
    return pl.pallas_call(
        outer_kernel,
        out_shape=pltpu.VMEM(ends.shape, jnp.float32),
        in_specs=[VMEM] * 4,
        out_specs=VMEM,
        scratch_shapes=[
            pltpu.VMEM(groups.shape, jnp.float32),
            pltpu.VMEM((max(count, groups.shape[0]), both // 2, LANES), jnp.float32),
        ],
        compiler_params=PARAMS,
        name="outer",
    )(near(ends), near(groups), near(red), near(top))


def exchanged(value, members):
    return lax.all_to_all(
        value, "gy", split_axis=0, concat_axis=0, tiled=True, axis_index_groups=members
    )


def finish_kernel(base_ref, near_ref, own_ref, out_hbm, left_t, right_t, out_t, sems):
    devices, both, _ = near_ref.shape
    share = both // 2
    turn = turned()
    for d in range(devices):
        left_t[pl.ds(d * share, share), :] = near_ref[d ^ turn, pl.ds(0, share), :]
        right_t[pl.ds(d * share, share), :] = near_ref[d ^ turn, pl.ds(share, share), :]
    left, right = left_t[...], right_t[...]
    copies = []
    for z in range(PLANES):
        here = pl.ds(z * ROWS, ROWS)
        from_left = own_ref[pl.ds(3 * PLANES + z, 1), :]
        from_right = own_ref[pl.ds(4 * PLANES + z, 1), :]
        out_t[here, :] = base_ref[here, :] + from_left * left + from_right * right
        if z % 4 == 3:
            part = pl.ds((z - 3) * ROWS, 4 * ROWS)
            copies.append(pltpu.make_async_copy(out_t.at[part], out_hbm.at[part], sems.at[z // 4]))
            copies[-1].start()
    for copy in copies:
        copy.wait()


def finish(base, sides, own):
    return pl.pallas_call(
        finish_kernel,
        out_shape=jax.ShapeDtypeStruct(base.shape, jnp.float32),
        in_specs=[VMEM] * 3,
        out_specs=ANY,
        scratch_shapes=[pltpu.VMEM((ROWS, LANES), jnp.float32)] * 2
        + [pltpu.VMEM((TILES, LANES), jnp.float32), pltpu.SemaphoreType.DMA((PLANES // 4,))],
        compiler_params=PARAMS,
        name="finish",
    )(near(base), near(sides), near(own))


def local(
    conc, target_one, target_two, diffusivity, src_shift, src_tile, interp_class, interp_mats
):
    devices = lax.axis_size("gy")
    as_stored = lambda value: value.transpose(0, 2, 1)
    list1, list2, place, shift, rows = request(as_stored(src_shift), as_stored(src_tile), to_rows(conc))
    asked2, asked1 = shifted(list2, "gx", -2), shifted(list1, "gx", -1)
    own, red, top, diag = coefficients(diffusivity, interp_mats, devices)
    got2 = shifted(serve(asked2, rows), "gx", 2)
    got1 = shifted(serve(asked1, rows), "gx", 1)
    dep, weights, to1, to2, one, two = before_arrival(
        place, rows, shift, as_stored(interp_class), diag, to_rows(target_one), to_rows(target_two)
    )
    dep = patched(to1, got1, dep)
    base, ends = slab(to2, got2, dep, weights, one, two, own)
    groups = devices // GROUP
    close = [[g * GROUP + k for k in range(GROUP)] for g in range(groups)]
    turn = [0 if g < groups // 2 else GROUP // 2 for g in range(groups)]
    distant = [[g * GROUP + (k ^ turn[g]) for g in range(groups)] for k in range(GROUP)]
    ends = exchanged(ends, close)
    sides = outer(ends, exchanged(inner(ends, red, groups), distant), red, top)
    sides = exchanged(sides, close)
    return from_rows(finish(base, sides, own), conc.shape)


def solution(mesh):
    slabs = P("gy", "gx", None)
    in_specs = (slabs, slabs, slabs, P(), slabs, slabs, slabs, P())
    return jax.shard_map(local, mesh=mesh, in_specs=in_specs, out_specs=slabs, check_vma=False)
```

```python
import jax
import jax.numpy as jnp
from jax import lax
from jax.experimental import pallas as pl
from jax.experimental.pallas import tpu as pltpu
from jax.sharding import PartitionSpec as P

LANES = 128
NMAT = 8
PLANES = 16
ROWS = 128
TILES = PLANES * ROWS
CAP = 512
GROUP = 8
HIGH = lax.Precision.HIGHEST
VMEM = pl.BlockSpec(memory_space=pltpu.VMEM)
SMEM = pl.BlockSpec(memory_space=pltpu.SMEM)
ANY = pl.BlockSpec(memory_space=pl.ANY)
PARAMS = pltpu.CompilerParams(vmem_limit_bytes=24 << 20)


def near(value):
    return pltpu.with_memory_space_constraint(value, pltpu.VMEM)


def shifted(value, axis, by):
    peers = lax.axis_size(axis)
    pairs = [(i, i + by) for i in range(peers) if 0 <= i + by < peers]
    return lax.ppermute(value, axis, pairs)


def far(value):
    return pltpu.with_memory_space_constraint(value, pltpu.HBM)


def to_rows(value):
    z, x, y = value.shape
    value = value.reshape(z, x // 8, 8, y // LANES, LANES).transpose(0, 1, 3, 2, 4)
    return value.reshape(z * x * (y // LANES), LANES)


def from_rows(rows, shape):
    z, x, y = shape
    rows = rows.reshape(z, x // 8, y // LANES, 8, LANES).transpose(0, 1, 3, 2, 4)
    return rows.reshape(shape)


def iota(shape, axis):
    return lax.broadcasted_iota(jnp.int32, shape, axis)


def by_lanes(ref):
    return jnp.concatenate([ref[:, b, :] for b in range(ref.shape[1])], axis=1)


def compact(shift, value, empty, picked_ref):
    before_lane = (iota((LANES, LANES), 0) < iota((LANES, LANES), 1)).astype(jnp.bfloat16)
    before_row = (iota((PLANES, PLANES), 1) < iota((PLANES, PLANES), 0)).astype(jnp.bfloat16)
    all_lanes = jnp.ones((LANES, LANES), jnp.bfloat16)
    for step in (1, 2):
        mine = shift == step
        mask = jnp.where(mine, 1.0, 0.0).astype(jnp.bfloat16)
        inside = jnp.dot(mask, before_lane, preferred_element_type=jnp.float32)
        per_row = jnp.dot(mask, all_lanes, preferred_element_type=jnp.float32)
        ahead = jnp.dot(before_row, per_row.astype(jnp.bfloat16), preferred_element_type=jnp.float32)
        rank = jnp.where(mine, (inside + ahead).astype(jnp.int32), -1)
        for block in range(CAP // 64):
            slot = iota((64, LANES), 0) + 64 * block
            picked = jnp.zeros((64, LANES), jnp.int32)
            for row in range(PLANES):
                picked = jnp.where(
                    rank[row : row + 1, :] == slot, value[row : row + 1, :] - empty, picked
                )
            picked_ref[pl.ds((step - 1) * CAP + 64 * block, 64), :] = picked
    picked = picked_ref[...]
    low = picked & 7
    total = jnp.full((8, 2 * CAP), empty, jnp.float32)
    for part in (picked - low, low):
        total = total + lax.dot_general(
            jnp.ones((8, LANES), jnp.bfloat16), part.astype(jnp.float32).astype(jnp.bfloat16),
            (((1,), (1,)), ((), ())), preferred_element_type=jnp.float32,
        )
    return total[0:1, :].astype(jnp.int32)


def request_kernel(
    shift_ref, tile_ref, rows_hbm, list1_ref, list2_ref, place_ref, shift_out, rows_ref, code_ref, picked_ref, sem
):
    copy = pltpu.make_async_copy(rows_hbm, rows_ref, sem)
    copy.start()
    code_ref[...] = shift_ref[...] * TILES + tile_ref[...]
    code = by_lanes(code_ref)
    shift, tile = lax.shift_right_logical(code, 11), code & (TILES - 1)
    place = (tile & -64) | ((tile & 7) << 3) | (lax.shift_right_logical(tile, 3) & 7)
    place_ref[...] = place
    shift_out[...] = shift
    both = compact(shift, place, 0, picked_ref)
    list1_ref[...] = both[:, :CAP]
    list2_ref[...] = both[:, CAP:]
    copy.wait()


def request(shift, tile, rows):
    return pl.pallas_call(
        request_kernel,
        out_shape=(
            pltpu.VMEM((1, CAP), jnp.int32),
            pltpu.VMEM((1, CAP), jnp.int32),
            jax.ShapeDtypeStruct((PLANES, LANES), jnp.int32),
            pltpu.VMEM((PLANES, LANES), jnp.int32),
            pltpu.VMEM((TILES, LANES), jnp.float32),
        ),
        in_specs=[VMEM] * 2 + [ANY],
        out_specs=[VMEM] * 5,
        scratch_shapes=[
            pltpu.VMEM(shift.shape, jnp.int32),
            pltpu.VMEM((2 * CAP, LANES), jnp.int32),
            pltpu.SemaphoreType.DMA,
        ],
        compiler_params=PARAMS,
        name="request",
    )(far(shift), far(tile), far(rows))


def serve_kernel(list_ref, rows_ref, out_ref):
    def step(k, carry):
        for j in range(128):
            slot = k * 128 + j
            out_ref[pl.ds(slot, 1), :] = rows_ref[pl.ds(list_ref[0, slot], 1), :]
        return carry

    lax.fori_loop(0, CAP // 128, step, 0)


def serve(wanted, rows):
    return pl.pallas_call(
        serve_kernel,
        out_shape=pltpu.VMEM((CAP, LANES), jnp.float32),
        in_specs=[SMEM, VMEM],
        out_specs=VMEM,
        compiler_params=PARAMS,
        name="serve",
    )(wanted, near(rows))


def coef_kernel(diff_ref, mats_ref, own_ref, red_ref, top_ref, diag_ref, own_t, row_t):
    devices = red_ref.shape[1]
    row = lambda a, z: a[z : z + 1, :]
    lane = iota((1, LANES), 1)
    plane_of = (iota((PLANES, LANES), 1) & (PLANES - 1)) == iota((PLANES, LANES), 0)
    diff = jnp.zeros((PLANES, LANES), jnp.float32)
    per_row = LANES // PLANES
    for r in range(diff_ref.shape[0]):
        goes = iota((LANES, LANES), 1) == lax.shift_right_logical(iota((LANES, LANES), 0), 4) + per_row * r
        diff = diff + jnp.dot(
            jnp.where(plane_of, diff_ref[pl.ds(r, 1), :], 0.0), jnp.where(goes, 1.0, 0.0),
            precision=HIGH, preferred_element_type=jnp.float32,
        )
    kr = [0.5 * (row(diff, z + 1) + row(diff, z)) for z in range(PLANES - 1)]
    beyond = pltpu.roll(diff, LANES - 1, 1)
    kr.append(jnp.where(lane < devices - 1, 0.5 * (row(beyond, 0) + row(diff, PLANES - 1)), 0.0))
    kl = [jnp.where(lane > 0, pltpu.roll(jnp.broadcast_to(kr[-1], (8, LANES)), 1, 1)[0:1, :], 0.0)]
    kl = kl + kr[:-1]
    inv, low, up = [], [], []
    for z in range(PLANES):
        pivot = 1.0 + kl[z] + kr[z]
        if z > 0:
            pivot = pivot - kr[z - 1] * up[z - 1]
        inv.append(1.0 / pivot)
        low.append(jnp.zeros_like(pivot) if z == 0 else kr[z - 1] * inv[z])
        up.append(kr[z] * inv[z])
    left = [kl[0] * inv[0]]
    for z in range(1, PLANES):
        left.append(low[z] * left[z - 1])
    right = [None] * PLANES
    right[-1] = up[-1]
    for z in range(PLANES - 2, -1, -1):
        left[z] = left[z] + up[z] * left[z + 1]
        right[z] = up[z] * right[z + 1]
    mine = lane == lax.axis_index("gy")
    ones = jnp.ones((LANES, LANES), jnp.float32)
    for kind, values in enumerate((inv, low, up, left, right)):
        for z in range(PLANES):
            own_t[pl.ds(kind * PLANES + z, 1), :] = jnp.where(mine, values[z], 0.0)
    own_ref[...] = jnp.dot(own_t[...], ones, precision=HIGH, preferred_element_type=jnp.float32)
    eye = iota((devices, LANES), 0) == iota((devices, LANES), 1)
    for kind, value in enumerate((left[0], left[-1], right[0], right[-1])):
        row_t[pl.ds(kind * devices, devices), :] = jnp.where(eye, value, 0.0)
    spread = jnp.dot(row_t[...], ones, precision=HIGH, preferred_element_type=jnp.float32)
    none, all_of = jnp.zeros((1, LANES), jnp.float32), jnp.ones((1, LANES), jnp.float32)
    groups = []
    for d in range(devices):
        if d % GROUP == 0:
            ratio, to_last, to_first, l_group = none, all_of, all_of, none
        l_first, l_last, r_first, r_last = (row(spread, kind * devices + d) for kind in range(4))
        gain = 1.0 / (1.0 - l_first * ratio)
        for kind, value in enumerate(
            (
                l_last * ratio * gain, l_last * gain, gain, gain * l_first, gain * r_first, ratio,
                to_first * gain, to_first * gain * l_first,
            )
        ):
            red_ref[kind, pl.ds(d, 1), :] = value
        l_group = l_group + to_first * gain * l_first * to_last
        to_first = to_first * gain * r_first
        ratio = r_last + l_last * ratio * gain * r_first
        to_last = l_last * gain * to_last
        if d % GROUP == GROUP - 1:
            groups.append((l_group, to_last, to_first, ratio))
    ratio = none
    for g, (l_first, l_last, r_first, r_last) in enumerate(groups):
        gain = 1.0 / (1.0 - l_first * ratio)
        for kind, value in enumerate(
            (l_last * ratio * gain, l_last * gain, gain, gain * l_first, gain * r_first, ratio)
        ):
            top_ref[kind, pl.ds(g, 1), :] = value
        ratio = r_last + l_last * ratio * gain * r_first
    r, c = iota((LANES, LANES), 0), iota((LANES, LANES), 1)
    for kind, at in enumerate((r == c, r == c + 1, r == c - 1)):
        values = jnp.concatenate(
            [jnp.sum(jnp.where(at, mats_ref[m], 0.0), axis=0, keepdims=True) for m in range(NMAT)], axis=0
        )
        first = values.astype(jnp.bfloat16).astype(jnp.float32)
        second = (values - first).astype(jnp.bfloat16).astype(jnp.float32)
        third = values - first - second
        stacked = jnp.concatenate([first, second, third, jnp.zeros_like(first)], axis=0)
        diag_ref[:, pl.ds(kind * LANES, LANES)] = stacked.astype(jnp.bfloat16)


def coefficients(diffusivity, mats, devices):
    return pl.pallas_call(
        coef_kernel,
        out_shape=(
            pltpu.VMEM((5 * PLANES, LANES), jnp.float32),
            pltpu.VMEM((8, devices, LANES), jnp.float32),
            pltpu.VMEM((6, devices // GROUP, LANES), jnp.float32),
            pltpu.VMEM((4 * NMAT, 3 * LANES), jnp.bfloat16),
        ),
        in_specs=[VMEM] * 2,
        out_specs=[VMEM] * 4,
        scratch_shapes=[
            pltpu.VMEM((5 * PLANES, LANES), jnp.float32),
            pltpu.VMEM((4 * devices, LANES), jnp.float32),
        ],
        compiler_params=PARAMS,
        cost_estimate=pl.CostEstimate(flops=8_000_000, bytes_accessed=4_000_000, transcendentals=0),
        name="coefficients",
    )(diffusivity.reshape(-1, LANES), mats)


def local_kernel(
    place_ref, rows_ref, shift_ref, class_ref, diag_ref, one_hbm, two_hbm,
    dep_ref, weights_ref, to1_ref, to2_ref, one_ref, two_ref, picked_ref, to_t, sems,
):
    copies = [
        pltpu.make_async_copy(one_hbm, one_ref, sems.at[0]),
        pltpu.make_async_copy(two_hbm, two_ref, sems.at[1]),
    ]
    for copy in copies:
        copy.start()
    shift = shift_ref[...]
    spot = iota((PLANES, LANES), 1)
    spot = ((spot & 8) << 3) | (lax.shift_right_logical(spot, 4) << 3) | (spot & 7)
    both = compact(shift, spot + ROWS * iota((PLANES, LANES), 0), TILES, picked_ref)
    to_t[...] = both
    copies = copies + [
        pltpu.make_async_copy(to_t.at[:, pl.ds(0, CAP)], to1_ref, sems.at[2]),
        pltpu.make_async_copy(to_t.at[:, pl.ds(CAP, CAP)], to2_ref, sems.at[3]),
    ]
    for copy in copies[2:]:
        copy.start()
    classes = by_lanes(class_ref)
    diag = diag_ref[...]
    of_class = jnp.bitwise_and(iota((4 * NMAT, ROWS), 0), NMAT - 1)
    for z in range(PLANES):
        chosen = jnp.where(of_class == classes[z : z + 1, :], 1.0, 0.0).astype(jnp.bfloat16)
        weights = lax.dot_general(
            chosen, diag, (((0,), (0,)), ((), ())), preferred_element_type=jnp.float32
        )
        for group in range(ROWS // 8):
            at = z * ROWS + (group % 2) * 64 + (group // 2) * 8
            weights_ref[pl.ds(at, 8), :] = weights[group * 8 : group * 8 + 8, :]

    def plane(z, carry):
        start = pl.multiple_of(z * ROWS, ROWS)
        for j in range(ROWS):
            at = ((j >> 3) & 1) * 64 + (j >> 4) * 8 + (j & 7)
            dep_ref[pl.ds(start + at, 1), :] = rows_ref[pl.ds(place_ref[z, j], 1), :]
        return carry

    lax.fori_loop(0, PLANES, plane, 0)
    for copy in copies:
        copy.wait()


def before_arrival(place, rows, shift, classes, diag, one, two):
    return pl.pallas_call(
        local_kernel,
        out_shape=(
            pltpu.VMEM((TILES + 8, LANES), jnp.float32),
            pltpu.VMEM((TILES, 3 * LANES), jnp.float32),
            pltpu.SMEM((1, CAP), jnp.int32),
            pltpu.SMEM((1, CAP), jnp.int32),
            pltpu.VMEM((TILES, LANES), jnp.float32),
            pltpu.VMEM((TILES, LANES), jnp.float32),
        ),
        in_specs=[SMEM] + [VMEM] * 4 + [ANY] * 2,
        out_specs=[VMEM] * 2 + [SMEM] * 2 + [VMEM] * 2,
        scratch_shapes=[
            pltpu.VMEM((2 * CAP, LANES), jnp.int32),
            pltpu.VMEM((1, 2 * CAP), jnp.int32),
            pltpu.SemaphoreType.DMA((4,)),
        ],
        compiler_params=PARAMS,
        cost_estimate=pl.CostEstimate(flops=20_000_000, bytes_accessed=10_000_000, transcendentals=0),
        name="before_arrival",
    )(place, near(rows), near(shift), classes, near(diag), far(one), far(two))


def turned():
    half = lax.axis_size("gy") // (2 * GROUP)
    return jnp.where(lax.axis_index("gy") // GROUP >= half, GROUP // 2, 0)


def patch_kernel(to_ref, got_ref, dep_in, dep_ref):
    del dep_in

    def patch(k, carry):
        start = pl.multiple_of(k * 32, 32)
        for j in range(32):
            dep_ref[pl.ds(to_ref[0, start + j], 1), :] = got_ref[pl.ds(start + j, 1), :]
        return carry

    lax.fori_loop(0, CAP // 32, patch, 0)


def patched(to, got, dep):
    return pl.pallas_call(
        patch_kernel,
        out_shape=pltpu.VMEM(dep.shape, jnp.float32),
        in_specs=[SMEM] + [VMEM] * 2,
        out_specs=VMEM,
        input_output_aliases={2: 0},
        compiler_params=PARAMS,
        name="patch",
    )(pltpu.with_memory_space_constraint(to, pltpu.SMEM), near(got), near(dep))


def slab_kernel(
    to_ref, got_ref, dep_in, weights_ref, one_ref, two_ref, own_ref, base_ref, ends_ref, dep_ref, partial
):
    patch_kernel(to_ref, got_ref, dep_in, dep_ref)

    def own(kind, z):
        return own_ref[pl.ds(kind * PLANES + z, 1), :]

    def forward(z, before):
        here = pl.ds(z * ROWS, ROWS)
        cells = dep_ref[here, :]
        adv = (
            weights_ref[here, pl.ds(0, LANES)] * cells
            + pltpu.roll(weights_ref[here, pl.ds(LANES, LANES)] * cells, 1, 1)
            + pltpu.roll(weights_ref[here, pl.ds(2 * LANES, LANES)] * cells, LANES - 1, 1)
        )
        a, b = 0.5 + adv, 2.0 + adv
        ab = a * b
        free = adv * ab / (ab + one_ref[here, :] * b + two_ref[here, :] * a)
        base_ref[here, :] = adv - free
        before = free * own(0, z) + before * own(1, z)
        partial[here, :] = before
        return before

    last = jnp.zeros((ROWS, LANES), jnp.float32)
    for z in range(PLANES):
        last = forward(z, last)

    def backward(k, after):
        z = PLANES - 1 - k
        here = pl.ds(z * ROWS, ROWS)
        after = partial[here, :] + after * own(2, z)
        base_ref[here, :] = base_ref[here, :] + after
        return after

    first = jnp.zeros((ROWS, LANES), jnp.float32)
    for k in range(PLANES):
        first = backward(k, first)
    share = ends_ref.shape[1] // 2
    turn = turned()
    for d in range(ends_ref.shape[0]):
        ends_ref[d ^ turn, pl.ds(0, share), :] = first[d * share : (d + 1) * share, :]
        ends_ref[d ^ turn, pl.ds(share, share), :] = last[d * share : (d + 1) * share, :]


def slab(to, got, dep, weights, one, two, own):
    base, ends, _ = pl.pallas_call(
        slab_kernel,
        out_shape=(
            pltpu.VMEM((TILES, LANES), jnp.float32),
            pltpu.VMEM((GROUP, 2 * ROWS // GROUP, LANES), jnp.float32),
            pltpu.VMEM((TILES + 8, LANES), jnp.float32),
        ),
        in_specs=[SMEM] + [VMEM] * 6,
        out_specs=[VMEM] * 3,
        scratch_shapes=[pltpu.VMEM((TILES, LANES), jnp.float32)],
        input_output_aliases={2: 2},
        compiler_params=PARAMS,
        name="slab",
    )(
        pltpu.with_memory_space_constraint(to, pltpu.SMEM), near(got), near(dep), near(weights), near(one), near(two), near(own))
    return base, ends


def inner_kernel(ends_ref, red_ref, out_ref):
    share = ends_ref.shape[1] // 2
    start = lax.axis_index("gy") // GROUP * GROUP
    coef = lambda kind, d: red_ref[kind, pl.ds(start + d, 1), :]
    top = last = jnp.zeros((share, LANES), jnp.float32)
    for d in range(GROUP):
        first = ends_ref[d, pl.ds(0, share), :]
        top = top + coef(6, d) * first + coef(7, d) * last
        last = ends_ref[d, pl.ds(share, share), :] + coef(0, d) * first + coef(1, d) * last
    for g in range(out_ref.shape[0]):
        out_ref[g, pl.ds(0, share), :] = top
        out_ref[g, pl.ds(share, share), :] = last


def inner(ends, red, groups):
    return pl.pallas_call(
        inner_kernel,
        out_shape=pltpu.VMEM((groups,) + ends.shape[1:], jnp.float32),
        in_specs=[VMEM] * 2,
        out_specs=VMEM,
        compiler_params=PARAMS,
        name="inner",
    )(near(ends), near(red))


def chain(ends_ref, coef, upto, after, carry_ref, put):
    count, both, _ = ends_ref.shape
    share = both // 2
    for d in range(count):
        first = ends_ref[d, pl.ds(0, share), :]
        carry_ref[d] = upto
        upto = ends_ref[d, pl.ds(share, share), :] + coef(0, d) * first + coef(1, d) * upto
    for d in range(count - 1, -1, -1):
        put(d, share, after)
        after = coef(2, d) * ends_ref[d, pl.ds(0, share), :] + coef(3, d) * carry_ref[d] + coef(4, d) * after
        put(d, 0, carry_ref[d] + coef(5, d) * after)


def outer_kernel(ends_ref, groups_ref, red_ref, top_ref, out_ref, sides_ref, carry_ref):
    share = ends_ref.shape[1] // 2
    group = lax.axis_index("gy") // GROUP
    zero = jnp.zeros((share, LANES), jnp.float32)

    def put_group(g, at, value):
        sides_ref[g, pl.ds(at, share), :] = value

    chain(groups_ref, lambda kind, g: top_ref[kind, pl.ds(g, 1), :], zero, zero, carry_ref, put_group)

    def put(d, at, value):
        out_ref[d, pl.ds(at, share), :] = value

    chain(
        ends_ref, lambda kind, d: red_ref[kind, pl.ds(group * GROUP + d, 1), :],
        sides_ref[group, pl.ds(0, share), :], sides_ref[group, pl.ds(share, share), :], carry_ref, put,
    )


def outer(ends, groups, red, top):
    count, both, _ = ends.shape
    return pl.pallas_call(
        outer_kernel,
        out_shape=pltpu.VMEM(ends.shape, jnp.float32),
        in_specs=[VMEM] * 4,
        out_specs=VMEM,
        scratch_shapes=[
            pltpu.VMEM(groups.shape, jnp.float32),
            pltpu.VMEM((max(count, groups.shape[0]), both // 2, LANES), jnp.float32),
        ],
        compiler_params=PARAMS,
        name="outer",
    )(near(ends), near(groups), near(red), near(top))


def exchanged(value, members):
    return lax.all_to_all(
        value, "gy", split_axis=0, concat_axis=0, tiled=True, axis_index_groups=members
    )


def finish_kernel(base_ref, near_ref, own_ref, out_hbm, left_t, right_t, out_t, sems):
    devices, both, _ = near_ref.shape
    share = both // 2
    turn = turned()
    for d in range(devices):
        left_t[pl.ds(d * share, share), :] = near_ref[d ^ turn, pl.ds(0, share), :]
        right_t[pl.ds(d * share, share), :] = near_ref[d ^ turn, pl.ds(share, share), :]
    left, right = left_t[...], right_t[...]
    copies = []
    for z in range(PLANES):
        here = pl.ds(z * ROWS, ROWS)
        from_left = own_ref[pl.ds(3 * PLANES + z, 1), :]
        from_right = own_ref[pl.ds(4 * PLANES + z, 1), :]
        out_t[here, :] = base_ref[here, :] + from_left * left + from_right * right
        if z % 4 == 3:
            part = pl.ds((z - 3) * ROWS, 4 * ROWS)
            copies.append(pltpu.make_async_copy(out_t.at[part], out_hbm.at[part], sems.at[z // 4]))
            copies[-1].start()
    for copy in copies:
        copy.wait()


def finish(base, sides, own):
    return pl.pallas_call(
        finish_kernel,
        out_shape=jax.ShapeDtypeStruct(base.shape, jnp.float32),
        in_specs=[VMEM] * 3,
        out_specs=ANY,
        scratch_shapes=[pltpu.VMEM((ROWS, LANES), jnp.float32)] * 2
        + [pltpu.VMEM((TILES, LANES), jnp.float32), pltpu.SemaphoreType.DMA((PLANES // 4,))],
        compiler_params=PARAMS,
        name="finish",
    )(near(base), near(sides), near(own))


def local(
    conc, target_one, target_two, diffusivity, src_shift, src_tile, interp_class, interp_mats
):
    devices = lax.axis_size("gy")
    as_stored = lambda value: value.transpose(0, 2, 1)
    list1, list2, place, shift, rows = request(as_stored(src_shift), as_stored(src_tile), to_rows(conc))
    asked2, asked1 = shifted(list2, "gx", -2), shifted(list1, "gx", -1)
    own, red, top, diag = coefficients(diffusivity, interp_mats, devices)
    got2 = shifted(serve(asked2, rows), "gx", 2)
    got1 = shifted(serve(asked1, rows), "gx", 1)
    dep, weights, to1, to2, one, two = before_arrival(
        place, rows, shift, as_stored(interp_class), diag, to_rows(target_one), to_rows(target_two)
    )
    dep = patched(to1, got1, dep)
    base, ends = slab(to2, got2, dep, weights, one, two, own)
    groups = devices // GROUP
    close = [[g * GROUP + k for k in range(GROUP)] for g in range(groups)]
    turn = [0 if g < groups // 2 else GROUP // 2 for g in range(groups)]
    distant = [[g * GROUP + (k ^ turn[g]) for g in range(groups)] for k in range(GROUP)]
    ends = exchanged(ends, close)
    sides = outer(ends, exchanged(inner(ends, red, groups), distant), red, top)
    sides = exchanged(sides, close)
    return from_rows(finish(base, sides, own), conc.shape)


def solution(mesh):
    slabs = P("gy", "gx", None)
    in_specs = (slabs, slabs, slabs, P(), slabs, slabs, slabs, P())
    return jax.shard_map(local, mesh=mesh, in_specs=in_specs, out_specs=slabs, check_vma=False)
```
